32 devices in a mesh: tm: 8 (over z, x), space: 4 (over y, core).
Axes of the slice: x: 2, y: 2, z: 4, core: 2. Of those that a mesh axis runs over, the one named last changes fastest.
Arguments:
- guess: float32 [8, 5, 2, 32, 64, 128], P('tm', None, None, 'space'), may hold values from 0 to 1
- feed_rate: float32 [32, 64, 128], P('space'), may hold values from 0.05 to 0.5
- kill_rate: float32 [32, 64, 128], P('space'), may hold values from 0.05 to 0.5
Outputs:
- end_state: float32 [8, 2, 32, 64, 128], P('tm', None, 'space')
- next_nodes: float32 [8, 5, 2, 32, 64, 128], P('tm', None, None, 'space')
The draws below stay inside these ranges and needn't reach their ends.
All inputs are finite; a program needn't handle non-finite values.
Results may differ from the reference program's by a relative error of at most 0.00002.
Values sent between devices are 32-bit elements; how exact they have to be, the bound alone decides.
A program may use at most 64 MiB of HBM per device.

```python
import math
import jax
import jax.numpy as jnp
import numpy as np
from jax import lax

NY = 64
NZ = 128
NODES = 5
SWEEPS = 4
NX = 32
SLABS = 8


def steps_of(rng, dims, shards, least, high):
    gain = 1.0
    for position, parts in shards:
        steps = jax.random.uniform(jax.random.fold_in(jax.random.fold_in(rng, 6), position), (parts,), jnp.float32, least / len(shards), high / len(shards))
        gain = gain * jnp.repeat(jnp.exp(steps), dims[position] // parts).reshape((-1,) + (1,) * (len(dims) - 1 - position))
    return gain


def setup_inputs(seed: int = 0) -> dict:
    splits = jax.random.split(jax.random.key(seed), 4)
    return {
        "guess": jnp.clip(1.0 * jax.random.uniform(splits[0], (SLABS, NODES, 2, NX, NY, NZ), jnp.float32) ** steps_of(splits[0], (SLABS, NODES, 2, NX, NY, NZ), ((0, 8), (3, 4)), -0.2, 0.2), 0.0, 1.0),
        "feed_rate": jnp.clip(jnp.exp(math.log(0.5) - 2.3025851 * jax.random.uniform(splits[1], (NX, NY, NZ), jnp.float32) ** steps_of(splits[1], (NX, NY, NZ), ((0, 4),), -0.2, 0.2)), 0.05, 0.5),
        "kill_rate": jnp.clip(jnp.exp(math.log(0.5) - 2.3025851 * jax.random.uniform(splits[2], (NX, NY, NZ), jnp.float32) ** steps_of(splits[2], (NX, NY, NZ), ((0, 4),), -0.2, 0.2)), 0.05, 0.5),
    }


substrate_spread = 0.2
catalyst_spread = 0.1
slab_time = 0.5

def lobatto_table():
    spread_root = math.sqrt(3.0 / 7.0)
    node_times = [0.0, (1.0 - spread_root) / 2.0, 0.5, (1.0 + spread_root) / 2.0, 1.0]
    table = [[0.0] * 5 for blank in range(5)]
    for column in range(5):
        coeffs = [1.0]
        divisor = 1.0
        for other_node in range(5):
            if other_node != column:
                product = [0.0] * (len(coeffs) + 1)
                for power, entry in enumerate(coeffs):
                    product[power + 1] += entry
                    product[power] -= node_times[other_node] * entry
                coeffs = product
                divisor *= node_times[column] - node_times[other_node]
        for row_index in range(5):
            upper = node_times[row_index]
            total_sum = 0.0
            for power, entry in enumerate(coeffs):
                total_sum += entry / (power + 1) * upper ** (power + 1)
            table[row_index][column] = total_sum / divisor
    return (np.array(node_times), np.array(table))

def laplacian(fields):
    total = -6.0 * fields
    for axis_id in (-3, -2, -1):
        total = total + jnp.roll(fields, 1, axis_id) + jnp.roll(fields, -1, axis_id)
    return total

def reaction_rates(fields, laplace_terms, feed_rate, kill_rate):
    substrate = fields[..., 0, :, :, :]
    catalyst = fields[..., 1, :, :, :]
    reacting = substrate * catalyst * catalyst
    grow_sub = substrate_spread * laplace_terms[..., 0, :, :, :] - reacting + feed_rate * (1.0 - substrate)
    grow_cat = catalyst_spread * laplace_terms[..., 1, :, :, :] + reacting - (feed_rate + kill_rate) * catalyst
    return jnp.stack([grow_sub, grow_cat], axis=-4)

def combine(start_pair, rates_all, weights):
    increment = jnp.zeros_like(rates_all)
    for column in range(weights.shape[1]):
        scale_col = jnp.asarray(weights[:, column], jnp.float32).reshape((-1, 1, 1, 1, 1))
        increment = increment + scale_col * rates_all[column][None]
    return start_pair[None] + slab_time * increment

def reference(guess, feed_rate, kill_rate):
    node_times, weights = lobatto_table()

    def sweep_slab(slab_pair):
        node_fields, start_pair = slab_pair
        rates_all = reaction_rates(node_fields, laplacian(node_fields), feed_rate, kill_rate)
        return combine(start_pair, rates_all, weights)
    node_all = guess
    for sweep_index in range(SWEEPS):
        end_fields = node_all[:, -1]
        starts = jnp.concatenate([guess[:1, 0], end_fields[:-1]], axis=0)
        node_all = lax.map(sweep_slab, (node_all, starts))
    end_state = node_all[:, -1]
    last_pair = end_state[-1]
    seed_rate = reaction_rates(last_pair, laplacian(last_pair), feed_rate, kill_rate)
    offsets = jnp.asarray(node_times, jnp.float32).reshape((-1, 1, 1, 1, 1))
    next_one = last_pair[None] + slab_time * offsets * seed_rate[None]
    next_nodes = jnp.broadcast_to(next_one[None], (SLABS,) + next_one.shape)
    return (end_state, next_nodes)
```

```python
import functools
import math

import jax
import jax.numpy as jnp
import numpy as np
from jax import lax
from jax.experimental import pallas as pl
from jax.experimental.pallas import tpu as pltpu
from jax.sharding import PartitionSpec as P

SWEEPS = 4
LAG = 2

substrate_spread = 0.2
catalyst_spread = 0.1
slab_time = 0.5

MESH = pl.DeviceIdType.MESH


def lobatto_table():
    spread_root = math.sqrt(3.0 / 7.0)
    node_times = [0.0, (1.0 - spread_root) / 2.0, 0.5, (1.0 + spread_root) / 2.0, 1.0]
    table = [[0.0] * 5 for blank in range(5)]
    for column in range(5):
        coeffs = [1.0]
        divisor = 1.0
        for other_node in range(5):
            if other_node != column:
                product = [0.0] * (len(coeffs) + 1)
                for power, entry in enumerate(coeffs):
                    product[power + 1] += entry
                    product[power] -= node_times[other_node] * entry
                coeffs = product
                divisor *= node_times[column] - node_times[other_node]
        for row_index in range(5):
            upper = node_times[row_index]
            total_sum = 0.0
            for power, entry in enumerate(coeffs):
                total_sum += entry / (power + 1) * upper ** (power + 1)
            table[row_index][column] = total_sum / divisor
    return (np.array(node_times), np.array(table))


def rates(below, here, above, feed, drain):
    rows, lanes = here[0].shape

    def lap(i):
        w = here[i]
        around = (pltpu.roll(w, 1, 0) + pltpu.roll(w, rows - 1, 0)) + (
            pltpu.roll(w, 1, 1) + pltpu.roll(w, lanes - 1, 1)
        )
        return around + (below[i] + above[i]) - 6.0 * w

    s, c = here
    reacting = s * c * c
    grow_sub = substrate_spread * lap(0) - reacting + feed * (1.0 - s)
    grow_cat = catalyst_spread * lap(1) + reacting - drain * c
    return grow_sub, grow_cat


def kernel(
    slabs, blocks, weights,
    guess, feed_in, kill_in,
    end_out, last_out, rate_out,
    u, last, feed, drain, fbuf,
    load_sem, fixed_sem, tm_send, tm_recv, halo_send, halo_recv, cast_send, cast_recv,
):
    layers = guess.shape[2]
    rows = guess.shape[3]
    tm = lax.axis_index("tm")
    sp = lax.axis_index("space")
    left = lax.rem(sp + blocks - 1, blocks)
    right = lax.rem(sp + 1, blocks)
    top = slabs // 2 - 1
    a = tm // 2
    b = tm % 2
    source = tm == slabs - 1
    not_source = tm < slabs - 1
    primary = 1 - b

    def layer_of(c):
        half = c // 2
        odd = c % 2
        return half + odd * (layers - 1 - 2 * half)

    loads = [
        pltpu.make_async_copy(guess, u.at[0, :, :, pl.ds(1, layers)], load_sem.at[0]),
        pltpu.make_async_copy(feed_in, feed, load_sem.at[1]),
        pltpu.make_async_copy(kill_in, drain, load_sem.at[2]),
    ]
    for load in loads:
        load.start()

    def fixed(k):
        return pltpu.make_async_copy(guess.at[0], u.at[k, 0, :, pl.ds(1, layers)], fixed_sem.at[k - 1])

    @pl.when(tm == 0)
    def _():
        for k in range(1, SWEEPS + 1):
            fixed(k).start()

    barrier = pltpu.get_barrier_semaphore()
    for hop in (1, 2, slabs - 2, slabs - 1):
        pl.semaphore_signal(barrier, inc=1, device_id={"tm": lax.rem(tm + hop, slabs)}, device_id_type=MESH)
    for side in (left, right):
        pl.semaphore_signal(barrier, inc=1, device_id={"space": side}, device_id_type=MESH)
    pl.semaphore_wait(barrier, 6)

    def stream(k, c, src):
        return pltpu.make_async_remote_copy(
            src_ref=src,
            dst_ref=u.at[k + 1, 0, :, 1 + layer_of(c)],
            send_sem=tm_send.at[k, c],
            recv_sem=tm_recv.at[k, c],
            device_id={"tm": lax.rem(tm + 1, slabs)},
            device_id_type=MESH,
        )

    def halo(k, side, src):
        return pltpu.make_async_remote_copy(
            src_ref=src,
            dst_ref=u.at[k, :, :, (1 - side) * (layers + 1)],
            send_sem=halo_send.at[k, side],
            recv_sem=halo_recv.at[k, side],
            device_id={"space": left + side * (right - left)},
            device_id_type=MESH,
        )

    def own_edge(k, side):
        return u.at[k, :, :, 1 + side * (layers - 1)]

    halo(0, 0, guess.at[:, :, 0]).start()
    halo(0, 1, guess.at[:, :, layers - 1]).start()

    @pl.when(not_source)
    def _():
        @pl.loop(0, layers)
        def _(c):
            stream(0, c, guess.at[4, :, layer_of(c)]).start()

    for load in loads:
        load.wait()
    drain[...] = drain[...] + feed[...]

    @pl.when(tm == 0)
    def _():
        for k in range(1, SWEEPS + 1):
            fixed(k).wait()

    def arrive(k, c):
        @pl.when(c == 0)
        def _():
            halo(k, 1, own_edge(k, 1)).wait_recv()

        @pl.when(c == 1)
        def _():
            halo(k, 0, own_edge(k, 0)).wait_recv()

    def begin(k, c):
        @pl.when(tm > 0)
        def _():
            stream(k, c, u.at[k, 4, :, 1 + layer_of(c)]).wait_recv()

    def all_rates(k, i):
        f, d = feed[i], drain[i]
        for j in range(5):
            below, here, above = ((u[k, j, 0, i + n], u[k, j, 1, i + n]) for n in range(3))
            fbuf[j, 0], fbuf[j, 1] = rates(below, here, above, f, d)

    def step(k, i, nodes):
        @pl.loop(0, rows // 8)
        def _(r):
            at = pl.ds(pl.multiple_of(r * 8, 8), 8)
            for s in range(2):
                start = u[k + 1, 0, s, 1 + i, at]
                grown = [fbuf[j, s, at] for j in range(5)]
                for m in nodes:
                    total = grown[0] * weights[m][0]
                    for j in range(1, 5):
                        total = total + grown[j] * weights[m][j]
                    u[k + 1, m, s, 1 + i, at] = start + total

    @pl.loop(0, SWEEPS - 1)
    def _(k):
        @pl.loop(0, layers)
        def _(c):
            i = layer_of(c)
            arrive(k, c)
            all_rates(k, i)
            begin(k, c)
            step(k, i, (4, 1, 2, 3))

            @pl.when(not_source)
            def _():
                stream(k + 1, c, u.at[k + 1, 4, :, 1 + i]).start()

            @pl.when(c < 2)
            def _():
                halo(k + 1, c, own_edge(k + 1, c)).start()

    def cast(lane, c, species, target):
        at = last.at[species, 1 + layer_of(c)]
        return pltpu.make_async_remote_copy(
            src_ref=at,
            dst_ref=at,
            send_sem=cast_send.at[lane, c],
            recv_sem=cast_recv.at[species, c],
            device_id={"tm": target},
            device_id_type=MESH,
        )

    down_on = a > 0
    cross_on = (a < top) | source
    cross_species = primary + jnp.where(source, 1, 0)
    extra_on = tm == 2 * (top - 1)

    def down(c):
        return cast(0, c, primary, lax.rem(tm + slabs - 2, slabs))

    def cross(c):
        return cast(1, c, cross_species, tm + 1 - 2 * b)

    def extra(c):
        return cast(2, c, 0, lax.rem(tm + 2, slabs))

    def last_halo(side):
        return pltpu.make_async_remote_copy(
            src_ref=last.at[:, 1 + side * (layers - 1)],
            dst_ref=last.at[:, (1 - side) * (layers + 1)],
            send_sem=halo_send.at[SWEEPS, side],
            recv_sem=halo_recv.at[SWEEPS, side],
            device_id={"space": left + side * (right - left)},
            device_id_type=MESH,
        )

    @pl.loop(0, layers + LAG)
    def _(c):
        @pl.when(c < layers)
        def _():
            i = layer_of(c)
            arrive(SWEEPS - 1, c)
            all_rates(SWEEPS - 1, i)
            begin(SWEEPS - 1, c)
            step(SWEEPS - 1, i, (4,))
            end_out[:, i] = u[SWEEPS, 4, :, 1 + i]

            @pl.when(source)
            def _():
                last[:, 1 + i] = u[SWEEPS, 4, :, 1 + i]

            @pl.when(not_source)
            def _():
                cast(0, c, primary, tm).wait_recv()

            @pl.when(down_on)
            def _():
                down(c).start()

            @pl.when(cross_on)
            def _():
                cross(c).start()

        @pl.when((c >= LAG) & extra_on)
        def _():
            late = c - LAG
            cast(0, late, 1 - primary, tm).wait_recv()
            extra(late).start()

    def rest(first, stop):
        @pl.when(not_source & (tm != 2 * (top - 1)))
        def _():
            @pl.loop(first, stop)
            def _(c):
                cast(0, c, 1 - primary, tm).wait_recv()

    rest(0, 2)
    last_halo(0).start()
    last_halo(1).start()
    rest(2, layers)
    last_halo(0).wait_recv()
    last_halo(1).wait_recv()

    @pl.loop(0, layers)
    def _(i):
        below, here, above = ((last[0, i + n], last[1, i + n]) for n in range(3))
        grow = rates(below, here, above, feed[i], drain[i])
        for s in range(2):
            last_out[s, i] = here[s]
            rate_out[s, i] = slab_time * grow[s]

    for k in range(SWEEPS):
        for side in range(2):
            halo(k, side, own_edge(k, side)).wait_send()
    last_halo(0).wait_send()
    last_halo(1).wait_send()

    @pl.loop(0, layers)
    def _(c):
        @pl.when(not_source)
        def _():
            for k in range(SWEEPS):
                stream(k, c, u.at[k, 4, :, 1 + layer_of(c)]).wait_send()

        @pl.when(down_on)
        def _():
            down(c).wait_send()

        @pl.when(cross_on)
        def _():
            cross(c).wait_send()

        @pl.when(extra_on)
        def _():
            extra(c).wait_send()


def finish(offsets, end, last, rate, end_hbm, next_hbm, nodes, sems, end_sem):
    layers = end.shape[1]
    end_copy = pltpu.make_async_copy(end, end_hbm, end_sem)

    def out(i):
        return pltpu.make_async_copy(nodes.at[:, :, i], next_hbm.at[:, :, i], sems.at[i])

    for i in range(layers):
        for s in range(2):
            base = last[s, i]
            grow = rate[s, i]
            for m in range(5):
                nodes[m, s, i] = base + offsets[m] * grow
        out(i).start()
    end_copy.start()
    for i in range(layers):
        out(i).wait()
    end_copy.wait()


def shards(slabs, blocks, guess, feed_rate, kill_rate):
    node_times, table = lobatto_table()
    weights = [[float(np.float32(slab_time * w)) for w in row] for row in table]
    _, nodes, species, layers, rows, lanes = guess.shape
    pair = jax.ShapeDtypeStruct((species, layers, rows, lanes), jnp.float32)
    dma = pltpu.SemaphoreType.DMA
    end, last, rate = pl.pallas_call(
        functools.partial(kernel, slabs, blocks, weights),
        out_shape=(pair, pair, pair),
        in_specs=[pl.BlockSpec(memory_space=pltpu.HBM)] * 3,
        out_specs=(pl.BlockSpec(memory_space=pltpu.VMEM),) * 3,
        scratch_shapes=[
            pltpu.VMEM((SWEEPS + 1, nodes, species, layers + 2, rows, lanes), jnp.float32),
            pltpu.VMEM((species, layers + 2, rows, lanes), jnp.float32),
            pltpu.VMEM((layers, rows, lanes), jnp.float32),
            pltpu.VMEM((layers, rows, lanes), jnp.float32),
            pltpu.VMEM((nodes, species, rows, lanes), jnp.float32),
            dma((3,)),
            dma((SWEEPS,)),
            dma((SWEEPS, layers)),
            dma((SWEEPS, layers)),
            dma((SWEEPS + 1, 2)),
            dma((SWEEPS + 1, 2)),
            dma((3, layers)),
            dma((2, layers)),
        ],
        compiler_params=pltpu.CompilerParams(
            collective_id=0, has_side_effects=True, vmem_limit_bytes=40 * 1024 * 1024
        ),
    )(*(pltpu.with_memory_space_constraint(x, pltpu.HBM) for x in (guess[0], feed_rate, kill_rate)))
    vmem = pl.BlockSpec(memory_space=pltpu.VMEM)
    hbm = pl.BlockSpec(memory_space=pltpu.HBM)
    end_state, next_nodes = pl.pallas_call(
        functools.partial(finish, [float(np.float32(t)) for t in node_times]),
        out_shape=(pair, jax.ShapeDtypeStruct((nodes, species, layers, rows, lanes), jnp.float32)),
        in_specs=[vmem] * 3,
        out_specs=(hbm, hbm),
        scratch_shapes=[
            pltpu.VMEM((nodes, species, layers, rows, lanes), jnp.float32),
            dma((layers,)),
            dma(()),
        ],
        compiler_params=pltpu.CompilerParams(vmem_limit_bytes=16 * 1024 * 1024),
    )(end, last, rate)
    return (end_state[None], next_nodes[None])


def solution(mesh):
    placed = (
        P("tm", None, None, "space", None, None),
        P("space", None, None),
        P("space", None, None),
    )
    return jax.shard_map(
        functools.partial(shards, mesh.shape["tm"], mesh.shape["space"]),
        mesh=mesh,
        in_specs=placed,
        out_specs=(P("tm", None, "space", None, None), P("tm", None, None, "space", None, None)),
        check_vma=False,
    )
```

```python
import functools
import math

import jax
import jax.numpy as jnp
import numpy as np
from jax import lax
from jax.experimental import pallas as pl
from jax.experimental.pallas import tpu as pltpu
from jax.sharding import PartitionSpec as P

SWEEPS = 4
LEAD = 1

substrate_spread = 0.2
catalyst_spread = 0.1
slab_time = 0.5

MESH = pl.DeviceIdType.MESH


def lobatto_table():
    spread_root = math.sqrt(3.0 / 7.0)
    node_times = [0.0, (1.0 - spread_root) / 2.0, 0.5, (1.0 + spread_root) / 2.0, 1.0]
    table = [[0.0] * 5 for blank in range(5)]
    for column in range(5):
        coeffs = [1.0]
        divisor = 1.0
        for other_node in range(5):
            if other_node != column:
                product = [0.0] * (len(coeffs) + 1)
                for power, entry in enumerate(coeffs):
                    product[power + 1] += entry
                    product[power] -= node_times[other_node] * entry
                coeffs = product
                divisor *= node_times[column] - node_times[other_node]
        for row_index in range(5):
            upper = node_times[row_index]
            total_sum = 0.0
            for power, entry in enumerate(coeffs):
                total_sum += entry / (power + 1) * upper ** (power + 1)
            table[row_index][column] = total_sum / divisor
    return (np.array(node_times), np.array(table))


def rates(below, here, above, feed, drain):
    rows, lanes = here[0].shape

    def lap(i):
        w = here[i]
        around = (pltpu.roll(w, 1, 0) + pltpu.roll(w, rows - 1, 0)) + (
            pltpu.roll(w, 1, 1) + pltpu.roll(w, lanes - 1, 1)
        )
        return around + (below[i] + above[i]) - 6.0 * w

    s, c = here
    reacting = s * c * c
    grow_sub = substrate_spread * lap(0) - reacting + feed * (1.0 - s)
    grow_cat = catalyst_spread * lap(1) + reacting - drain * c
    return grow_sub, grow_cat


def kernel(
    slabs, blocks, weights,
    guess, feed_in, kill_in,
    end_out, last_out, rate_out,
    u, last, inc, bay, feed, drain, fbuf,
    load_sem, fixed_sem, tm_send, tm_recv, halo_send, halo_recv,
    inc_send, inc_recv, bay_send, bay_recv, cast_send, cast_recv,
):
    layers = guess.shape[2]
    rows = guess.shape[3]
    final = SWEEPS - 1
    tm = lax.axis_index("tm")
    sp = lax.axis_index("space")
    left = lax.rem(sp + blocks - 1, blocks)
    right = lax.rem(sp + 1, blocks)
    source = tm == slabs - 1
    not_source = tm < slabs - 1
    second = tm == slabs - 2
    odd = tm % 2
    detoured = tm == slabs - 3

    def layer_of(c):
        half = c // 2
        flip = c % 2
        return half + flip * (layers - 1 - 2 * half)

    loads = [
        pltpu.make_async_copy(guess, u.at[0, :, :, pl.ds(1, layers)], load_sem.at[0]),
        pltpu.make_async_copy(feed_in, feed, load_sem.at[1]),
        pltpu.make_async_copy(kill_in, drain, load_sem.at[2]),
    ]

    def fixed(k):
        return pltpu.make_async_copy(guess.at[0], u.at[k, 0, :, pl.ds(1, layers)], fixed_sem.at[k - 1])

    barrier = pltpu.get_barrier_semaphore()
    for hop in (1, 2, 3, slabs - 3, slabs - 2, slabs - 1):
        pl.semaphore_signal(barrier, inc=1, device_id={"tm": lax.rem(tm + hop, slabs)}, device_id_type=MESH)
    for side in (left, right):
        pl.semaphore_signal(barrier, inc=1, device_id={"space": side}, device_id_type=MESH)

    for load in loads:
        load.start()

    @pl.when(tm == 0)
    def _():
        for k in range(1, SWEEPS + 1):
            fixed(k).start()

    pl.semaphore_wait(barrier, 8)

    def stream(k, c, src):
        return pltpu.make_async_remote_copy(
            src_ref=src,
            dst_ref=u.at[k + 1, 0, :, 1 + layer_of(c)],
            send_sem=tm_send.at[k, c],
            recv_sem=tm_recv.at[k, c],
            device_id={"tm": lax.rem(tm + 1, slabs)},
            device_id_type=MESH,
        )

    def detour(c):
        return pltpu.make_async_remote_copy(
            src_ref=u.at[final, 4, :, 1 + layer_of(c)],
            dst_ref=bay.at[:, layer_of(c)],
            send_sem=tm_send.at[final, c],
            recv_sem=bay_recv.at[c],
            device_id={"tm": 0},
            device_id_type=MESH,
        )

    def onward(c):
        return pltpu.make_async_remote_copy(
            src_ref=bay.at[:, layer_of(c)],
            dst_ref=u.at[SWEEPS, 0, :, 1 + layer_of(c)],
            send_sem=bay_send.at[c],
            recv_sem=tm_recv.at[final, c],
            device_id={"tm": slabs - 2},
            device_id_type=MESH,
        )

    def halo(k, side, src):
        return pltpu.make_async_remote_copy(
            src_ref=src,
            dst_ref=u.at[k, :, :, (1 - side) * (layers + 1)],
            send_sem=halo_send.at[k, side],
            recv_sem=halo_recv.at[k, side],
            device_id={"space": left + side * (right - left)},
            device_id_type=MESH,
        )

    def own_edge(k, side):
        return u.at[k, :, :, 1 + side * (layers - 1)]

    halo(0, 0, guess.at[:, :, 0]).start()
    halo(0, 1, guess.at[:, :, layers - 1]).start()

    @pl.when(not_source)
    def _():
        @pl.loop(0, layers)
        def _(c):
            stream(0, c, guess.at[4, :, layer_of(c)]).start()

    for load in loads:
        load.wait()
    drain[...] = drain[...] + feed[...]

    @pl.when(tm == 0)
    def _():
        for k in range(1, SWEEPS + 1):
            fixed(k).wait()

    def arrive(k, c):
        @pl.when(c == 0)
        def _():
            halo(k, 1, own_edge(k, 1)).wait_recv()

        @pl.when(c == 1)
        def _():
            halo(k, 0, own_edge(k, 0)).wait_recv()

    def begin(k, c):
        @pl.when(tm > 0)
        def _():
            stream(k, c, u.at[k, 4, :, 1 + layer_of(c)]).wait_recv()

    def all_rates(k, i):
        f, d = feed[i], drain[i]
        for j in range(5):
            below, here, above = ((u[k, j, 0, i + n], u[k, j, 1, i + n]) for n in range(3))
            fbuf[j, 0], fbuf[j, 1] = rates(below, here, above, f, d)

    def growth(grown, m):
        total = grown[0] * weights[m][0]
        for j in range(1, 5):
            total = total + grown[j] * weights[m][j]
        return total

    def step(k, i, nodes):
        @pl.loop(0, rows // 8)
        def _(r):
            at = pl.ds(pl.multiple_of(r * 8, 8), 8)
            for s in range(2):
                start = u[k + 1, 0, s, 1 + i, at]
                grown = [fbuf[j, s, at] for j in range(5)]
                for m in nodes:
                    u[k + 1, m, s, 1 + i, at] = start + growth(grown, m)

    def send_inc(c):
        at = inc.at[:, layer_of(c)]
        return pltpu.make_async_remote_copy(
            src_ref=at,
            dst_ref=at,
            send_sem=inc_send.at[c],
            recv_sem=inc_recv.at[c],
            device_id={"tm": slabs - 2},
            device_id_type=MESH,
        )

    def early(p):
        inner = jnp.where(p < layers - 4, p + 2, p - (layers - 4))
        return jnp.where(p < layers - 2, inner, p)

    def foresee(c):
        i = layer_of(c)
        arrive(final, c)
        all_rates(final, i)

        @pl.loop(0, rows // 8)
        def _(r):
            at = pl.ds(pl.multiple_of(r * 8, 8), 8)
            for s in range(2):
                inc[s, i, at] = growth([fbuf[j, s, at] for j in range(5)], 4)

        send_inc(c).start()

    @pl.loop(0, final)
    def _(k):
        @pl.loop(0, layers)
        def _(c):
            i = layer_of(c)
            arrive(k, c)
            all_rates(k, i)
            begin(k, c)
            step(k, i, (4, 1, 2, 3))
            aside = detoured & (k == final - 1)

            @pl.when(not_source & jnp.logical_not(aside))
            def _():
                stream(k + 1, c, u.at[k + 1, 4, :, 1 + i]).start()

            @pl.when(aside)
            def _():
                detour(c).start()

            @pl.when(c < 2)
            def _():
                halo(k + 1, c, own_edge(k + 1, c)).start()

            @pl.when(source & (k == final - 1) & (c >= 4))
            def _():
                @pl.loop(c - 4, jnp.where(c == layers - 1, layers, c - 3))
                def _(p):
                    foresee(early(p))

    def cast(s, c, target):
        at = last.at[s, 1 + layer_of(c)]
        return pltpu.make_async_remote_copy(
            src_ref=at,
            dst_ref=at,
            send_sem=cast_send.at[s, c],
            recv_sem=cast_recv.at[s, c],
            device_id={"tm": target},
            device_id_type=MESH,
        )

    def down(s, c):
        return cast(s, c, lax.rem(tm + slabs - 2, slabs))

    hops = (slabs - 1 - tm) // 2 - jnp.where(odd == 0, LEAD, 0)
    lag = jnp.where(tm == 0, layers, jnp.minimum(2 * hops, layers))

    def last_halo(side):
        return pltpu.make_async_remote_copy(
            src_ref=last.at[:, 1 + side * (layers - 1)],
            dst_ref=last.at[:, (1 - side) * (layers + 1)],
            send_sem=halo_send.at[SWEEPS, side],
            recv_sem=halo_recv.at[SWEEPS, side],
            device_id={"space": left + side * (right - left)},
            device_id_type=MESH,
        )

    def last_rate(c):
        i = layer_of(c)
        below, here, above = ((last[0, i + n], last[1, i + n]) for n in range(3))
        grow = rates(below, here, above, feed[i], drain[i])
        for s in range(2):
            last_out[s, i] = here[s]
            rate_out[s, i] = slab_time * grow[s]

    def pass_on(p):
        c = jnp.where(odd == 1, p, early(p))
        for s in range(2):
            @pl.when(tm < slabs - 2)
            def _():
                cast(s, c, tm).wait_recv()

            @pl.when(tm >= 2)
            def _():
                down(s, c).start()

        @pl.when(c == 1)
        def _():
            last_halo(0).start()
            last_halo(1).start()

        @pl.when((p >= layers - 4) & (p < layers - 1))
        def _():
            last_rate(p - layers + 6)

    @pl.when(second)
    def _():
        @pl.loop(0, layers)
        def _(p):
            i = layer_of(early(p))
            send_inc(early(p)).wait_recv()
            last[:, 1 + i] = u[final, 4, :, 1 + i] + inc[:, i]
            pass_on(p)

    @pl.loop(0, 2 * layers)
    def _(t):
        @pl.when((tm < slabs - 2) & (t >= lag) & (t < lag + layers))
        def _():
            pass_on(t - lag)

        @pl.when((tm == 0) & (t < layers))
        def _():
            detour(t).wait_recv()
            onward(t).start()

        @pl.when(not_source & (t < layers))
        def _():
            i = layer_of(t)
            arrive(final, t)
            all_rates(final, i)
            begin(final, t)
            step(final, i, (4,))
            end_out[:, i] = u[SWEEPS, 4, :, 1 + i]

        @pl.when(source & (t < layers))
        def _():
            i = layer_of(t)
            begin(final, t)
            now = u[SWEEPS, 0, :, 1 + i] + inc[:, i]
            last[:, 1 + i] = now
            end_out[:, i] = now
            pass_on(t)

    last_halo(0).wait_recv()
    last_halo(1).wait_recv()

    @pl.loop(0, layers - 3)
    def _(j):
        last_rate(jnp.where(j < 2, j, j + 3))

    for k in range(SWEEPS):
        for side in range(2):
            halo(k, side, own_edge(k, side)).wait_send()
    last_halo(0).wait_send()
    last_halo(1).wait_send()

    @pl.loop(0, layers)
    def _(c):
        @pl.when(not_source)
        def _():
            for k in range(SWEEPS):
                stream(k, c, u.at[k, 4, :, 1 + layer_of(c)]).wait_send()

        @pl.when(source)
        def _():
            send_inc(c).wait_send()

        @pl.when(tm == 0)
        def _():
            onward(c).wait_send()

        @pl.when(tm >= 2)
        def _():
            for s in range(2):
                down(s, c).wait_send()


def finish(offsets, end, last, rate, end_hbm, next_hbm, nodes, sems, end_sem):
    layers = end.shape[1]
    end_copy = pltpu.make_async_copy(end, end_hbm, end_sem)

    def out(i):
        return pltpu.make_async_copy(nodes.at[:, :, i], next_hbm.at[:, :, i], sems.at[i])

    for i in range(layers):
        for s in range(2):
            base = last[s, i]
            grow = rate[s, i]
            for m in range(5):
                nodes[m, s, i] = base + offsets[m] * grow
        out(i).start()
    end_copy.start()
    for i in range(layers):
        out(i).wait()
    end_copy.wait()


def shards(slabs, blocks, guess, feed_rate, kill_rate):
    node_times, table = lobatto_table()
    weights = [[float(np.float32(slab_time * w)) for w in row] for row in table]
    offsets = [float(np.float32(t)) for t in node_times]
    _, nodes, species, layers, rows, lanes = guess.shape
    pair = jax.ShapeDtypeStruct((species, layers, rows, lanes), jnp.float32)
    dma = pltpu.SemaphoreType.DMA
    vmem = pl.BlockSpec(memory_space=pltpu.VMEM)
    hbm = pl.BlockSpec(memory_space=pltpu.HBM)
    end, last, rate = pl.pallas_call(
        functools.partial(kernel, slabs, blocks, weights),
        out_shape=(pair,) * 3,
        in_specs=[hbm] * 3,
        out_specs=(vmem,) * 3,
        scratch_shapes=[
            pltpu.VMEM((SWEEPS + 1, nodes, species, layers + 2, rows, lanes), jnp.float32),
            pltpu.VMEM((species, layers + 2, rows, lanes), jnp.float32),
            pltpu.VMEM((species, layers, rows, lanes), jnp.float32),
            pltpu.VMEM((species, layers, rows, lanes), jnp.float32),
            pltpu.VMEM((layers, rows, lanes), jnp.float32),
            pltpu.VMEM((layers, rows, lanes), jnp.float32),
            pltpu.VMEM((nodes, species, rows, lanes), jnp.float32),
            dma((3,)),
            dma((SWEEPS,)),
            dma((SWEEPS, layers)),
            dma((SWEEPS, layers)),
            dma((SWEEPS + 1, 2)),
            dma((SWEEPS + 1, 2)),
            dma((layers,)),
            dma((layers,)),
            dma((layers,)),
            dma((layers,)),
            dma((species, layers)),
            dma((species, layers)),
        ],
        compiler_params=pltpu.CompilerParams(
            collective_id=0, has_side_effects=True, vmem_limit_bytes=40 * 1024 * 1024
        ),
    )(*(pltpu.with_memory_space_constraint(x, pltpu.HBM) for x in (guess[0], feed_rate, kill_rate)))
    end_state, next_nodes = pl.pallas_call(
        functools.partial(finish, offsets),
        out_shape=(pair, jax.ShapeDtypeStruct((nodes, species, layers, rows, lanes), jnp.float32)),
        in_specs=[vmem] * 3,
        out_specs=(hbm, hbm),
        scratch_shapes=[
            pltpu.VMEM((nodes, species, layers, rows, lanes), jnp.float32),
            dma((layers,)),
            dma(()),
        ],
        compiler_params=pltpu.CompilerParams(vmem_limit_bytes=16 * 1024 * 1024),
    )(end, last, rate)
    return (end_state[None], next_nodes[None])


def solution(mesh):
    placed = (
        P("tm", None, None, "space", None, None),
        P("space", None, None),
        P("space", None, None),
    )
    return jax.shard_map(
        functools.partial(shards, mesh.shape["tm"], mesh.shape["space"]),
        mesh=mesh,
        in_specs=placed,
        out_specs=(P("tm", None, "space", None, None), P("tm", None, None, "space", None, None)),
        check_vma=False,
    )
```

```python
import functools
import math

import jax
import jax.numpy as jnp
import numpy as np
from jax import lax
from jax.experimental import pallas as pl
from jax.experimental.pallas import tpu as pltpu
from jax.sharding import PartitionSpec as P

SWEEPS = 4
FIRST = (2, 1)
TAILS = (3, 3)

substrate_spread = 0.2
catalyst_spread = 0.1
slab_time = 0.5

MESH = pl.DeviceIdType.MESH


def lobatto_table():
    spread_root = math.sqrt(3.0 / 7.0)
    node_times = [0.0, (1.0 - spread_root) / 2.0, 0.5, (1.0 + spread_root) / 2.0, 1.0]
    table = [[0.0] * 5 for blank in range(5)]
    for column in range(5):
        coeffs = [1.0]
        divisor = 1.0
        for other_node in range(5):
            if other_node != column:
                product = [0.0] * (len(coeffs) + 1)
                for power, entry in enumerate(coeffs):
                    product[power + 1] += entry
                    product[power] -= node_times[other_node] * entry
                coeffs = product
                divisor *= node_times[column] - node_times[other_node]
        for row_index in range(5):
            upper = node_times[row_index]
            total_sum = 0.0
            for power, entry in enumerate(coeffs):
                total_sum += entry / (power + 1) * upper ** (power + 1)
            table[row_index][column] = total_sum / divisor
    return (np.array(node_times), np.array(table))


def rates(below, here, above, feed, drain):
    rows, lanes = here[0].shape

    def lap(i):
        w = here[i]
        around = (pltpu.roll(w, 1, 0) + pltpu.roll(w, rows - 1, 0)) + (
            pltpu.roll(w, 1, 1) + pltpu.roll(w, lanes - 1, 1)
        )
        return around + (below[i] + above[i]) - 6.0 * w

    s, c = here
    reacting = s * c * c
    grow_sub = substrate_spread * lap(0) - reacting + feed * (1.0 - s)
    grow_cat = catalyst_spread * lap(1) + reacting - drain * c
    return grow_sub, grow_cat


def kernel(
    slabs, blocks, weights,
    guess, feed_in, kill_in,
    end_out, last_out, rate_out,
    u, last, inc, bay, feed, drain, fbuf,
    load_sem, fixed_sem, tm_send, tm_recv, halo_send, halo_recv, edge_send,
    inc_send, inc_recv, bay_send, bay_recv, cast_send, back_send, far_send, cast_recv,
):
    layers = guess.shape[2]
    rows = guess.shape[3]
    final = SWEEPS - 1
    tm = lax.axis_index("tm")
    sp = lax.axis_index("space")
    left = lax.rem(sp + blocks - 1, blocks)
    right = lax.rem(sp + 1, blocks)
    source = tm == slabs - 1
    not_source = tm < slabs - 1
    second = tm == slabs - 2
    odd = tm % 2
    detoured = tm == slabs - 3

    def layer_of(c):
        return jnp.where(c < 2, c * (layers - 1), c - 1)

    loads = [
        pltpu.make_async_copy(guess, u.at[0, :, :, pl.ds(1, layers)], load_sem.at[0]),
        pltpu.make_async_copy(feed_in, feed, load_sem.at[1]),
        pltpu.make_async_copy(kill_in, drain, load_sem.at[2]),
    ]

    def fixed(k):
        return pltpu.make_async_copy(guess.at[0], u.at[k, 0, :, pl.ds(1, layers)], fixed_sem.at[k - 1])

    barrier = pltpu.get_barrier_semaphore()
    jumps = (1, 2, 3, 2 * min(2, slabs // 2 - 1))
    greeted = sorted({n % slabs for n in jumps} | {-n % slabs for n in jumps})
    for hop in greeted:
        pl.semaphore_signal(barrier, inc=1, device_id={"tm": lax.rem(tm + hop, slabs)}, device_id_type=MESH)
    for side in (left, right):
        pl.semaphore_signal(barrier, inc=1, device_id={"space": side}, device_id_type=MESH)

    for load in loads:
        load.start()

    @pl.when(tm == 0)
    def _():
        for k in range(1, SWEEPS + 1):
            fixed(k).start()

    pl.semaphore_wait(barrier, len(greeted) + 2)

    def stream(k, c, src):
        return pltpu.make_async_remote_copy(
            src_ref=src,
            dst_ref=u.at[k + 1, 0, :, 1 + layer_of(c)],
            send_sem=tm_send.at[k],
            recv_sem=tm_recv.at[k, c],
            device_id={"tm": lax.rem(tm + 1, slabs)},
            device_id_type=MESH,
        )

    def detour(k, c):
        return pltpu.make_async_remote_copy(
            src_ref=u.at[k, 4, :, 1 + layer_of(c)],
            dst_ref=bay.at[k // 2, :, layer_of(c)],
            send_sem=tm_send.at[k],
            recv_sem=bay_recv.at[k // 2, c],
            device_id={"tm": 0},
            device_id_type=MESH,
        )

    def onward(k, c):
        return pltpu.make_async_remote_copy(
            src_ref=bay.at[k // 2, :, layer_of(c)],
            dst_ref=u.at[k + 1, 0, :, 1 + layer_of(c)],
            send_sem=bay_send.at[k // 2],
            recv_sem=tm_recv.at[k, c],
            device_id={"tm": slabs - 2},
            device_id_type=MESH,
        )

    def halo(k, side, src):
        return pltpu.make_async_remote_copy(
            src_ref=src,
            dst_ref=u.at[k, :, :, (1 - side) * (layers + 1)],
            send_sem=halo_send,
            recv_sem=halo_recv.at[k, side],
            device_id={"space": left + side * (right - left)},
            device_id_type=MESH,
        )

    def own_edge(k, side):
        return u.at[k, :, :, 1 + side * (layers - 1)]

    halo(0, 0, guess.at[:, :, 0]).start()
    halo(0, 1, guess.at[:, :, layers - 1]).start()

    @pl.when(not_source)
    def _():
        @pl.loop(0, layers)
        def _(c):
            stream(0, c, guess.at[4, :, layer_of(c)]).start()

    for load in loads:
        load.wait()
    drain[...] = drain[...] + feed[...]

    @pl.when(tm == 0)
    def _():
        for k in range(1, SWEEPS + 1):
            fixed(k).wait()

    def arrive(k, c):
        @pl.when(c == 0)
        def _():
            halo(k, 1, own_edge(k, 1)).wait_recv()

        @pl.when(c == 1)
        def _():
            halo(k, 0, own_edge(k, 0)).wait_recv()

    def begin(k, c):
        @pl.when(tm > 0)
        def _():
            stream(k, c, u.at[k, 4, :, 1 + layer_of(c)]).wait_recv()

    def all_rates(k, i):
        f, d = feed[i], drain[i]
        for j in range(5):
            below, here, above = ((u[k, j, 0, i + n], u[k, j, 1, i + n]) for n in range(3))
            fbuf[j, 0], fbuf[j, 1] = rates(below, here, above, f, d)

    def growth(grown, m):
        total = grown[0] * weights[m][0]
        for j in range(1, 5):
            total = total + grown[j] * weights[m][j]
        return total

    def step(k, i, nodes):
        @pl.loop(0, rows // 8)
        def _(r):
            at = pl.ds(pl.multiple_of(r * 8, 8), 8)
            for s in range(2):
                start = u[k + 1, 0, s, 1 + i, at]
                grown = [fbuf[j, s, at] for j in range(5)]
                for m in nodes:
                    u[k + 1, m, s, 1 + i, at] = start + growth(grown, m)

    def send_inc(c):
        at = inc.at[:, layer_of(c)]
        return pltpu.make_async_remote_copy(
            src_ref=at,
            dst_ref=at,
            send_sem=inc_send,
            recv_sem=inc_recv.at[c],
            device_id={"tm": slabs - 2},
            device_id_type=MESH,
        )

    def early(p):
        inner = jnp.where(p < layers - 4, p + 2, p - (layers - 4))
        return jnp.where(p < layers - 2, inner, p)

    def foresee(c):
        i = layer_of(c)
        arrive(final, c)
        all_rates(final, i)

        @pl.loop(0, rows // 8)
        def _(r):
            at = pl.ds(pl.multiple_of(r * 8, 8), 8)
            for s in range(2):
                inc[s, i, at] = growth([fbuf[j, s, at] for j in range(5)], 4)

        send_inc(c).start()

    depth = slabs // 2 - 1
    place = (slabs - 1 - tm) // 2
    entry = jnp.where(odd == 1, min(FIRST[1], depth), min(FIRST[0], depth))
    rooted = place == 0
    leads = rooted | ((place >= entry) & (place < depth))
    backs = (place >= 2) & (place <= entry)

    def cast(s, c, send, hop):
        at = last.at[s, 1 + layer_of(c)]
        return pltpu.make_async_remote_copy(
            src_ref=at,
            dst_ref=at,
            send_sem=send,
            recv_sem=cast_recv.at[s, c],
            device_id={"tm": lax.rem(tm + slabs + hop, slabs)},
            device_id_type=MESH,
        )

    def down(s, c):
        return cast(s, c, cast_send, jnp.where(rooted, -2 * entry, -2))

    def back(s, c):
        return cast(s, c, back_send, 2)

    paired = slabs >= 8 and min(FIRST[0], depth) == 2
    near, deep = TAILS if paired else (0, 0)
    gives = (tm == 0) | (tm == slabs - 3)
    spares_down = tm == 3
    spares_back = tm == slabs - 6

    def across(s, c):
        return cast(s, c, far_send, jnp.where(tm == 0, 1, -1))

    def last_halo(side):
        return pltpu.make_async_remote_copy(
            src_ref=last.at[:, 1 + side * (layers - 1)],
            dst_ref=last.at[:, (1 - side) * (layers + 1)],
            send_sem=edge_send,
            recv_sem=halo_recv.at[SWEEPS, side],
            device_id={"space": left + side * (right - left)},
            device_id_type=MESH,
        )

    def chunk(p):
        return jnp.where(odd == 1, p, early(p))

    def relay(p):
        c = chunk(p)
        for s in range(2):
            @pl.when(tm < slabs - 2)
            def _():
                down(s, c).wait_recv()

            @pl.when(leads & jnp.logical_not(spares_down & (c >= layers - near)))
            def _():
                down(s, c).start()

            @pl.when(backs & jnp.logical_not(spares_back & (c >= layers - deep)))
            def _():
                back(s, c).start()

            @pl.when(gives & (c >= layers - jnp.where(tm == 0, near, deep)))
            def _():
                across(s, c).start()

        @pl.when(c == 1)
        def _():
            last_halo(0).start()
            last_halo(1).start()

    @pl.loop(0, final)
    def _(k):
        @pl.loop(0, layers)
        def _(c):
            i = layer_of(c)

            arrive(k, c)
            all_rates(k, i)
            begin(k, c)
            step(k, i, (4, 1, 2, 3))
            away = detoured & ((k == final - 1) | ((k == 0) & (c >= layers // 2)))


            @pl.when(not_source & jnp.logical_not(away))
            def _():
                stream(k + 1, c, u.at[k + 1, 4, :, 1 + i]).start()

            @pl.when(away)
            def _():
                detour(k + 1, c).start()

            @pl.when(c < 2)
            def _():
                halo(k + 1, c, own_edge(k + 1, c)).start()

            @pl.when((tm == 0) & (k == 0) & (c == layers - 1))
            def _():
                @pl.loop(layers // 2, layers)
                def _(b):
                    detour(1, b).wait_recv()
                    onward(1, b).start()

            @pl.when(source & (k == final - 1) & (c >= 3))
            def _():
                @pl.loop(c - 3, jnp.where(c == layers - 1, layers - 2, c - 2))
                def _(p):
                    foresee(early(p))

    steps = 1 + jnp.where(place > entry, place - entry, entry - place)
    lag = jnp.where(tm == 0, layers, jnp.minimum(2 * steps - 2 + 2 * odd, layers))

    def last_rate(c):
        i = layer_of(c)
        below, here, above = ((last[0, i + n], last[1, i + n]) for n in range(3))
        grow = rates(below, here, above, feed[i], drain[i])
        for s in range(2):
            last_out[s, i] = here[s]
            rate_out[s, i] = slab_time * grow[s]

    def settled(j):
        plain = jnp.where(j < layers - 2, j + 2, j - layers + 2)
        return jnp.where(odd == 1, plain, mixed(j))

    def mixed(j):
        return jnp.where(j < 2, j + 3, jnp.where(j < 3, 2, jnp.where(j < layers - 2, j + 2, j - layers + 2)))

    @pl.when(tm == 0)
    def _():
        @pl.loop(0, layers)
        def _(c):
            detour(final, c).wait_recv()
            onward(final, c).start()

    @pl.when(second)
    def _():
        @pl.loop(0, layers)
        def _(p):
            i = layer_of(early(p))
            send_inc(early(p)).wait_recv()
            last[:, 1 + i] = u[final, 4, :, 1 + i] + inc[:, i]
            relay(p)

    ready = jnp.where(tm < slabs - 2, layers - 4, 0)

    @pl.loop(0, 2 * layers)
    def _(t):
        p = t - lag

        @pl.when((tm < slabs - 2) & (p >= 0) & (p < layers))
        def _():
            relay(p)

            gap = jnp.where(odd == 1, 2, layers - 3)

            @pl.when((p >= 2) & (p < layers - 1) & (p != gap))
            def _():
                last_rate(settled(p - 2 - jnp.where(p > gap, 1, 0)))

        @pl.when(not_source & (t < layers))
        def _():
            i = layer_of(t)
            arrive(final, t)
            all_rates(final, i)
            begin(final, t)
            step(final, i, (4,))
            end_out[:, i] = u[SWEEPS, 4, :, 1 + i]

        @pl.when(source & (t < layers))
        def _():
            i = layer_of(t)

            @pl.when(t == 2)
            def _():
                @pl.loop(layers - 2, layers)
                def _(c):
                    foresee(c)

            begin(final, t)
            now = u[SWEEPS, 0, :, 1 + i] + inc[:, i]
            last[:, 1 + i] = now
            end_out[:, i] = now
            relay(t)

    last_halo(0).wait_recv()
    last_halo(1).wait_recv()

    @pl.loop(ready, layers)
    def _(j):
        last_rate(settled(j))

    def drain_sends(ref, sem):
        pltpu.make_async_copy(ref, ref, sem).wait()

    drain_sends(u.at[pl.ds(0, SWEEPS), :, :, pl.ds(1, 2)], halo_send)
    drain_sends(last.at[:, pl.ds(1, 2)], edge_send)
    whole = last.at[:, pl.ds(1, layers)]

    @pl.when(not_source)
    def _():
        for k in range(SWEEPS):
            drain_sends(whole, tm_send.at[k])

    @pl.when(source)
    def _():
        drain_sends(whole, inc_send)

    @pl.when(tm == 0)
    def _():
        drain_sends(whole, bay_send.at[1])
        drain_sends(last.at[:, pl.ds(1, layers - layers // 2)], bay_send.at[0])

    @pl.when(leads & jnp.logical_not(spares_down))
    def _():
        drain_sends(whole, cast_send)

    @pl.when(leads & spares_down)
    def _():
        drain_sends(last.at[:, pl.ds(1, layers - near)], cast_send)

    @pl.when(backs & jnp.logical_not(spares_back))
    def _():
        drain_sends(whole, back_send)

    @pl.when(backs & spares_back)
    def _():
        drain_sends(last.at[:, pl.ds(1, layers - deep)], back_send)

    if paired:
        @pl.when(tm == 0)
        def _():
            drain_sends(last.at[:, pl.ds(1, near)], far_send)

        @pl.when(tm == slabs - 3)
        def _():
            drain_sends(last.at[:, pl.ds(1, deep)], far_send)


def finish(offsets, end, last, rate, end_hbm, next_hbm, nodes, sems, start_sem, end_sem):
    layers = end.shape[1]
    start_copy = pltpu.make_async_copy(last, next_hbm.at[0], start_sem)
    end_copy = pltpu.make_async_copy(end, end_hbm, end_sem)
    start_copy.start()
    end_copy.start()

    def out(i):
        return pltpu.make_async_copy(nodes.at[:, :, i], next_hbm.at[pl.ds(1, 4), :, i], sems.at[i])

    for i in range(layers):
        for s in range(2):
            base = last[s, i]
            grow = rate[s, i]
            for m in range(1, 5):
                nodes[m - 1, s, i] = base + offsets[m] * grow
        out(i).start()
    for i in range(layers):
        out(i).wait()
    start_copy.wait()
    end_copy.wait()


def shards(slabs, blocks, guess, feed_rate, kill_rate):
    node_times, table = lobatto_table()
    weights = [[float(np.float32(slab_time * w)) for w in row] for row in table]
    offsets = [float(np.float32(t)) for t in node_times]
    _, nodes, species, layers, rows, lanes = guess.shape
    pair = jax.ShapeDtypeStruct((species, layers, rows, lanes), jnp.float32)
    dma = pltpu.SemaphoreType.DMA
    vmem = pl.BlockSpec(memory_space=pltpu.VMEM)
    hbm = pl.BlockSpec(memory_space=pltpu.HBM)
    end, last, rate = pl.pallas_call(
        functools.partial(kernel, slabs, blocks, weights),
        out_shape=(pair,) * 3,
        in_specs=[hbm] * 3,
        out_specs=(vmem,) * 3,
        scratch_shapes=[
            pltpu.VMEM((SWEEPS + 1, nodes, species, layers + 2, rows, lanes), jnp.float32),
            pltpu.VMEM((species, layers + 2, rows, lanes), jnp.float32),
            pltpu.VMEM((species, layers, rows, lanes), jnp.float32),
            pltpu.VMEM((2, species, layers, rows, lanes), jnp.float32),
            pltpu.VMEM((layers, rows, lanes), jnp.float32),
            pltpu.VMEM((layers, rows, lanes), jnp.float32),
            pltpu.VMEM((nodes, species, rows, lanes), jnp.float32),
            dma((3,)),
            dma((SWEEPS,)),
            dma((SWEEPS,)),
            dma((SWEEPS, layers)),
            dma(()),
            dma((SWEEPS + 1, 2)),
            dma(()),
            dma(()),
            dma((layers,)),
            dma((2,)),
            dma((2, layers)),
            dma(()),
            dma(()),
            dma(()),
            dma((species, layers)),
        ],
        compiler_params=pltpu.CompilerParams(
            collective_id=0, has_side_effects=True, vmem_limit_bytes=40 * 1024 * 1024
        ),
    )(*(pltpu.with_memory_space_constraint(x, pltpu.HBM) for x in (guess[0], feed_rate, kill_rate)))
    end_state, next_nodes = pl.pallas_call(
        functools.partial(finish, offsets),
        out_shape=(pair, jax.ShapeDtypeStruct((nodes, species, layers, rows, lanes), jnp.float32)),
        in_specs=[vmem] * 3,
        out_specs=(hbm, hbm),
        scratch_shapes=[
            pltpu.VMEM((nodes - 1, species, layers, rows, lanes), jnp.float32),
            dma((layers,)),
            dma(()),
            dma(()),
        ],
        compiler_params=pltpu.CompilerParams(vmem_limit_bytes=16 * 1024 * 1024),
    )(end, last, rate)
    return (end_state[None], next_nodes[None])


def solution(mesh):
    placed = (
        P("tm", None, None, "space", None, None),
        P("space", None, None),
        P("space", None, None),
    )
    return jax.shard_map(
        functools.partial(shards, mesh.shape["tm"], mesh.shape["space"]),
        mesh=mesh,
        in_specs=placed,
        out_specs=(P("tm", None, "space", None, None), P("tm", None, None, "space", None, None)),
        check_vma=False,
    )
```

```python
import functools
import math

import jax
import jax.numpy as jnp
import numpy as np
from jax import lax
from jax.experimental import pallas as pl
from jax.experimental.pallas import tpu as pltpu
from jax.sharding import PartitionSpec as P

SWEEPS = 4
FIRST = (2, 1)
NEAR = 4
DEEP = 2

substrate_spread = 0.2
catalyst_spread = 0.1
slab_time = 0.5

MESH = pl.DeviceIdType.MESH


def lobatto_table():
    spread_root = math.sqrt(3.0 / 7.0)
    node_times = [0.0, (1.0 - spread_root) / 2.0, 0.5, (1.0 + spread_root) / 2.0, 1.0]
    table = [[0.0] * 5 for blank in range(5)]
    for column in range(5):
        coeffs = [1.0]
        divisor = 1.0
        for other_node in range(5):
            if other_node != column:
                product = [0.0] * (len(coeffs) + 1)
                for power, entry in enumerate(coeffs):
                    product[power + 1] += entry
                    product[power] -= node_times[other_node] * entry
                coeffs = product
                divisor *= node_times[column] - node_times[other_node]
        for row_index in range(5):
            upper = node_times[row_index]
            total_sum = 0.0
            for power, entry in enumerate(coeffs):
                total_sum += entry / (power + 1) * upper ** (power + 1)
            table[row_index][column] = total_sum / divisor
    return (np.array(node_times), np.array(table))


def rates(below, here, above, feed, drain):
    rows, lanes = here[0].shape

    def lap(i):
        w = here[i]
        around = (pltpu.roll(w, 1, 0) + pltpu.roll(w, rows - 1, 0)) + (
            pltpu.roll(w, 1, 1) + pltpu.roll(w, lanes - 1, 1)
        )
        return around + (below[i] + above[i]) - 6.0 * w

    s, c = here
    reacting = s * c * c
    grow_sub = substrate_spread * lap(0) - reacting + feed * (1.0 - s)
    grow_cat = catalyst_spread * lap(1) + reacting - drain * c
    return grow_sub, grow_cat


def kernel(
    slabs, blocks, weights,
    guess, feed_in, kill_in,
    end_out, last_out, rate_out,
    u, last, inc, bay, feed, drain, fbuf,
    load_sem, fixed_sem, tm_send, tm_recv, halo_send, halo_recv, edge_send,
    inc_send, inc_recv, bay_send, bay_recv, cast_send, back_send, far_send, cast_recv,
):
    layers = guess.shape[2]
    rows = guess.shape[3]
    final = SWEEPS - 1
    tm = lax.axis_index("tm")
    sp = lax.axis_index("space")
    left = lax.rem(sp + blocks - 1, blocks)
    right = lax.rem(sp + 1, blocks)
    source = tm == slabs - 1
    not_source = tm < slabs - 1
    second = tm == slabs - 2
    odd = tm % 2
    detoured = tm == slabs - 3

    def layer_of(c):
        return jnp.where(c < 2, c * (layers - 1), c - 1)

    loads = [
        pltpu.make_async_copy(guess, u.at[0, :, :, pl.ds(1, layers)], load_sem.at[0]),
        pltpu.make_async_copy(feed_in, feed, load_sem.at[1]),
        pltpu.make_async_copy(kill_in, drain, load_sem.at[2]),
    ]

    def fixed(k):
        return pltpu.make_async_copy(guess.at[0], u.at[k, 0, :, pl.ds(1, layers)], fixed_sem.at[k - 1])

    barrier = pltpu.get_barrier_semaphore()
    jumps = (1, 2, 3, 2 * min(2, slabs // 2 - 1))
    greeted = sorted({n % slabs for n in jumps} | {-n % slabs for n in jumps})
    for hop in greeted:
        pl.semaphore_signal(barrier, inc=1, device_id={"tm": lax.rem(tm + hop, slabs)}, device_id_type=MESH)
    for side in (left, right):
        pl.semaphore_signal(barrier, inc=1, device_id={"space": side}, device_id_type=MESH)

    for load in loads:
        load.start()

    @pl.when(tm == 0)
    def _():
        for k in range(1, SWEEPS + 1):
            fixed(k).start()

    pl.semaphore_wait(barrier, len(greeted) + 2)

    def stream(k, c, src):
        return pltpu.make_async_remote_copy(
            src_ref=src,
            dst_ref=u.at[k + 1, 0, :, 1 + layer_of(c)],
            send_sem=tm_send.at[k],
            recv_sem=tm_recv.at[k, c],
            device_id={"tm": lax.rem(tm + 1, slabs)},
            device_id_type=MESH,
        )

    def detour(k, c):
        return pltpu.make_async_remote_copy(
            src_ref=u.at[k, 4, :, 1 + layer_of(c)],
            dst_ref=bay.at[k // 2, :, layer_of(c)],
            send_sem=tm_send.at[k],
            recv_sem=bay_recv.at[k // 2, c],
            device_id={"tm": 0},
            device_id_type=MESH,
        )

    def onward(k, c):
        return pltpu.make_async_remote_copy(
            src_ref=bay.at[k // 2, :, layer_of(c)],
            dst_ref=u.at[k + 1, 0, :, 1 + layer_of(c)],
            send_sem=bay_send.at[k // 2],
            recv_sem=tm_recv.at[k, c],
            device_id={"tm": slabs - 2},
            device_id_type=MESH,
        )

    def halo(k, side, src):
        return pltpu.make_async_remote_copy(
            src_ref=src,
            dst_ref=u.at[k, :, :, (1 - side) * (layers + 1)],
            send_sem=halo_send,
            recv_sem=halo_recv.at[k, side],
            device_id={"space": left + side * (right - left)},
            device_id_type=MESH,
        )

    def own_edge(k, side):
        return u.at[k, :, :, 1 + side * (layers - 1)]

    halo(0, 0, guess.at[:, :, 0]).start()
    halo(0, 1, guess.at[:, :, layers - 1]).start()

    @pl.when(not_source)
    def _():
        @pl.loop(0, layers)
        def _(c):
            stream(0, c, guess.at[4, :, layer_of(c)]).start()

    for load in loads:
        load.wait()
    drain[...] = drain[...] + feed[...]

    @pl.when(tm == 0)
    def _():
        for k in range(1, SWEEPS + 1):
            fixed(k).wait()

    def arrive(k, c):
        @pl.when(c == 0)
        def _():
            halo(k, 1, own_edge(k, 1)).wait_recv()

        @pl.when(c == 1)
        def _():
            halo(k, 0, own_edge(k, 0)).wait_recv()

    def begin(k, c):
        @pl.when(tm > 0)
        def _():
            stream(k, c, u.at[k, 4, :, 1 + layer_of(c)]).wait_recv()

    def all_rates(k, i):
        f, d = feed[i], drain[i]
        for j in range(5):
            below, here, above = ((u[k, j, 0, i + n], u[k, j, 1, i + n]) for n in range(3))
            fbuf[j, 0], fbuf[j, 1] = rates(below, here, above, f, d)

    def growth(grown, m):
        total = grown[0] * weights[m][0]
        for j in range(1, 5):
            total = total + grown[j] * weights[m][j]
        return total

    def step(k, i, nodes):
        @pl.loop(0, rows // 8)
        def _(r):
            at = pl.ds(pl.multiple_of(r * 8, 8), 8)
            for s in range(2):
                start = u[k + 1, 0, s, 1 + i, at]
                grown = [fbuf[j, s, at] for j in range(5)]
                for m in nodes:
                    u[k + 1, m, s, 1 + i, at] = start + growth(grown, m)

    def send_inc(c):
        at = inc.at[:, layer_of(c)]
        return pltpu.make_async_remote_copy(
            src_ref=at,
            dst_ref=at,
            send_sem=inc_send,
            recv_sem=inc_recv.at[c],
            device_id={"tm": slabs - 2},
            device_id_type=MESH,
        )

    def early(p):
        inner = jnp.where(p < layers - 3, p + 2, p - (layers - 3))
        return jnp.where(p < layers - 1, inner, p)

    def foresee(c):
        i = layer_of(c)
        arrive(final, c)
        all_rates(final, i)

        @pl.loop(0, rows // 8)
        def _(r):
            at = pl.ds(pl.multiple_of(r * 8, 8), 8)
            for s in range(2):
                inc[s, i, at] = growth([fbuf[j, s, at] for j in range(5)], 4)

        send_inc(c).start()

    depth = slabs // 2 - 1
    place = (slabs - 1 - tm) // 2
    entry = jnp.where(odd == 1, min(FIRST[1], depth), min(FIRST[0], depth))
    rooted = place == 0
    leads = rooted | ((place >= entry) & (place < depth))
    backs = (place >= 2) & (place <= entry)

    def cast(s, c, send, hop):
        at = last.at[s, 1 + layer_of(c)]
        return pltpu.make_async_remote_copy(
            src_ref=at,
            dst_ref=at,
            send_sem=send,
            recv_sem=cast_recv.at[s, c],
            device_id={"tm": lax.rem(tm + slabs + hop, slabs)},
            device_id_type=MESH,
        )

    def down(s, c):
        return cast(s, c, cast_send, jnp.where(rooted, -2 * entry, -2))

    def back(s, c):
        return cast(s, c, back_send, 2)

    paired = slabs >= 8 and min(FIRST[0], depth) == 2
    near = NEAR if paired else 0
    deep = DEEP if paired else 0
    spares_down = tm == 3
    spares_back = tm == slabs - 6

    def nearby(c):
        return c >= layers - near

    def offside(c):
        return (c < deep) | (c >= layers - deep)

    def across(s, c):
        return cast(s, c, far_send, jnp.where(tm == 0, 1, -1))

    def last_halo(side):
        return pltpu.make_async_remote_copy(
            src_ref=last.at[:, 1 + side * (layers - 1)],
            dst_ref=last.at[:, (1 - side) * (layers + 1)],
            send_sem=edge_send,
            recv_sem=halo_recv.at[SWEEPS, side],
            device_id={"space": left + side * (right - left)},
            device_id_type=MESH,
        )

    plain = jnp.where((tm == slabs - 4) & paired, 1, odd)

    def chunk(p):
        return jnp.where(plain == 1, p, early(p))

    def relay(p):
        c = chunk(p)
        for s in range(2):
            @pl.when(tm < slabs - 2)
            def _():
                down(s, c).wait_recv()

            @pl.when(leads & jnp.logical_not(spares_down & nearby(c)))
            def _():
                down(s, c).start()

            @pl.when(backs & jnp.logical_not(spares_back & offside(c)))
            def _():
                back(s, c).start()

            @pl.when(((tm == 0) & nearby(c)) | ((tm == slabs - 3) & offside(c)))
            def _():
                across(s, c).start()

        @pl.when(c == 0)
        def _():
            last_halo(0).start()

        @pl.when(c == 1)
        def _():
            last_halo(1).start()

    @pl.loop(0, final)
    def _(k):
        @pl.loop(0, layers)
        def _(c):
            i = layer_of(c)

            arrive(k, c)
            all_rates(k, i)
            begin(k, c)
            step(k, i, (4, 1, 2, 3))
            away = detoured & ((k == final - 1) | ((k == 0) & (c >= layers // 2)))


            @pl.when(not_source & jnp.logical_not(away))
            def _():
                stream(k + 1, c, u.at[k + 1, 4, :, 1 + i]).start()

            @pl.when(away)
            def _():
                detour(k + 1, c).start()

            @pl.when(c < 2)
            def _():
                halo(k + 1, c, own_edge(k + 1, c)).start()

            @pl.when((tm == 0) & (k == 0) & (c == layers - 1))
            def _():
                @pl.loop(layers // 2, layers)
                def _(b):
                    detour(1, b).wait_recv()
                    onward(1, b).start()

            @pl.when(source & (k == final - 1) & (c >= 3))
            def _():
                @pl.loop(c - 3, jnp.where(c == layers - 1, layers - 1, c - 2))
                def _(p):
                    foresee(early(p))

    steps = 1 + jnp.where(place > entry, place - entry, entry - place)
    lag = jnp.where(tm == 0, layers, jnp.minimum(2 * steps - 2 + 2 * odd, layers))

    def last_rate(c):
        i = layer_of(c)
        below, here, above = ((last[0, i + n], last[1, i + n]) for n in range(3))
        grow = rates(below, here, above, feed[i], drain[i])
        for s in range(2):
            last_out[s, i] = here[s]
            rate_out[s, i] = slab_time * grow[s]

    def settled(j):
        swapped = jnp.where(j < 3, j + 3, jnp.where(j < 4, 2, j + 2))
        return jnp.where(plain == 1, j + 2, swapped)

    @pl.when(tm == 0)
    def _():
        @pl.loop(0, layers)
        def _(c):
            detour(final, c).wait_recv()
            onward(final, c).start()

    @pl.when(second)
    def _():
        @pl.loop(0, layers)
        def _(p):
            i = layer_of(early(p))
            send_inc(early(p)).wait_recv()
            last[:, 1 + i] = u[final, 4, :, 1 + i] + inc[:, i]
            relay(p)

    ready = jnp.where(tm < slabs - 2, layers - 4, 0)

    @pl.loop(0, 2 * layers)
    def _(t):
        p = t - lag

        @pl.when((tm < slabs - 2) & (p >= 0) & (p < layers))
        def _():
            relay(p)

            @pl.when((p >= 2 + plain) & (p < layers - 2 + plain))
            def _():
                last_rate(settled(p - 2 - plain))

        @pl.when(not_source & (t < layers))
        def _():
            i = layer_of(t)
            arrive(final, t)
            all_rates(final, i)
            begin(final, t)
            step(final, i, (4,))
            end_out[:, i] = u[SWEEPS, 4, :, 1 + i]

        @pl.when(source & (t < layers))
        def _():
            i = layer_of(t)

            @pl.when(t == 2)
            def _():
                foresee(layers - 1)

            begin(final, t)
            now = u[SWEEPS, 0, :, 1 + i] + inc[:, i]
            last[:, 1 + i] = now
            end_out[:, i] = now
            relay(t)

    @pl.loop(ready, layers - 2)
    def _(j):
        last_rate(settled(j))

    last_halo(0).wait_recv()
    last_halo(1).wait_recv()

    @pl.loop(0, 2)
    def _(c):
        last_rate(c)

    def drain_sends(ref, sem):
        pltpu.make_async_copy(ref, ref, sem).wait()

    drain_sends(u.at[pl.ds(0, SWEEPS), :, :, pl.ds(1, 2)], halo_send)
    drain_sends(last.at[:, pl.ds(1, 2)], edge_send)
    whole = last.at[:, pl.ds(1, layers)]

    @pl.when(not_source)
    def _():
        for k in range(SWEEPS):
            drain_sends(whole, tm_send.at[k])

    @pl.when(source)
    def _():
        drain_sends(whole, inc_send)

    @pl.when(tm == 0)
    def _():
        drain_sends(whole, bay_send.at[1])
        drain_sends(last.at[:, pl.ds(1, layers - layers // 2)], bay_send.at[0])

    @pl.when(leads & jnp.logical_not(spares_down))
    def _():
        drain_sends(whole, cast_send)

    @pl.when(leads & spares_down)
    def _():
        drain_sends(last.at[:, pl.ds(1, layers - near)], cast_send)

    @pl.when(backs & jnp.logical_not(spares_back))
    def _():
        drain_sends(whole, back_send)

    @pl.when(backs & spares_back)
    def _():
        drain_sends(last.at[:, pl.ds(1, layers - 2 * deep)], back_send)

    if paired:
        @pl.when(tm == 0)
        def _():
            drain_sends(last.at[:, pl.ds(1, near)], far_send)

        @pl.when(tm == slabs - 3)
        def _():
            drain_sends(last.at[:, pl.ds(1, 2 * deep)], far_send)


def finish(offsets, end, last, rate, end_hbm, next_hbm, nodes, sems, start_sem, end_sem):
    layers = end.shape[1]
    start_copy = pltpu.make_async_copy(last, next_hbm.at[0], start_sem)
    end_copy = pltpu.make_async_copy(end, end_hbm, end_sem)
    start_copy.start()
    end_copy.start()

    def out(i):
        return pltpu.make_async_copy(nodes.at[:, :, i], next_hbm.at[pl.ds(1, 4), :, i], sems.at[i])

    for i in range(layers):
        for s in range(2):
            base = last[s, i]
            grow = rate[s, i]
            for m in range(1, 5):
                nodes[m - 1, s, i] = base + offsets[m] * grow
        out(i).start()
    for i in range(layers):
        out(i).wait()
    start_copy.wait()
    end_copy.wait()


def shards(slabs, blocks, guess, feed_rate, kill_rate):
    node_times, table = lobatto_table()
    weights = [[float(np.float32(slab_time * w)) for w in row] for row in table]
    offsets = [float(np.float32(t)) for t in node_times]
    _, nodes, species, layers, rows, lanes = guess.shape
    pair = jax.ShapeDtypeStruct((species, layers, rows, lanes), jnp.float32)
    dma = pltpu.SemaphoreType.DMA
    vmem = pl.BlockSpec(memory_space=pltpu.VMEM)
    hbm = pl.BlockSpec(memory_space=pltpu.HBM)
    end, last, rate = pl.pallas_call(
        functools.partial(kernel, slabs, blocks, weights),
        out_shape=(pair,) * 3,
        in_specs=[hbm] * 3,
        out_specs=(vmem,) * 3,
        scratch_shapes=[
            pltpu.VMEM((SWEEPS + 1, nodes, species, layers + 2, rows, lanes), jnp.float32),
            pltpu.VMEM((species, layers + 2, rows, lanes), jnp.float32),
            pltpu.VMEM((species, layers, rows, lanes), jnp.float32),
            pltpu.VMEM((2, species, layers, rows, lanes), jnp.float32),
            pltpu.VMEM((layers, rows, lanes), jnp.float32),
            pltpu.VMEM((layers, rows, lanes), jnp.float32),
            pltpu.VMEM((nodes, species, rows, lanes), jnp.float32),
            dma((3,)),
            dma((SWEEPS,)),
            dma((SWEEPS,)),
            dma((SWEEPS, layers)),
            dma(()),
            dma((SWEEPS + 1, 2)),
            dma(()),
            dma(()),
            dma((layers,)),
            dma((2,)),
            dma((2, layers)),
            dma(()),
            dma(()),
            dma(()),
            dma((species, layers)),
        ],
        compiler_params=pltpu.CompilerParams(
            collective_id=0, has_side_effects=True, vmem_limit_bytes=40 * 1024 * 1024
        ),
    )(*(pltpu.with_memory_space_constraint(x, pltpu.HBM) for x in (guess[0], feed_rate, kill_rate)))
    end_state, next_nodes = pl.pallas_call(
        functools.partial(finish, offsets),
        out_shape=(pair, jax.ShapeDtypeStruct((nodes, species, layers, rows, lanes), jnp.float32)),
        in_specs=[vmem] * 3,
        out_specs=(hbm, hbm),
        scratch_shapes=[
            pltpu.VMEM((nodes - 1, species, layers, rows, lanes), jnp.float32),
            dma((layers,)),
            dma(()),
            dma(()),
        ],
        compiler_params=pltpu.CompilerParams(vmem_limit_bytes=16 * 1024 * 1024),
    )(end, last, rate)
    return (end_state[None], next_nodes[None])


def solution(mesh):
    placed = (
        P("tm", None, None, "space", None, None),
        P("space", None, None),
        P("space", None, None),
    )
    return jax.shard_map(
        functools.partial(shards, mesh.shape["tm"], mesh.shape["space"]),
        mesh=mesh,
        in_specs=placed,
        out_specs=(P("tm", None, "space", None, None), P("tm", None, None, "space", None, None)),
        check_vma=False,
    )
```

```python
import functools
import math

import jax
import jax.numpy as jnp
import numpy as np
from jax import lax
from jax.experimental import pallas as pl
from jax.experimental.pallas import tpu as pltpu
from jax.sharding import PartitionSpec as P

SWEEPS = 4
SIDE = 1
FIRST = (2, 1)
NEAR = 4
DEEP = 2

substrate_spread = 0.2
catalyst_spread = 0.1
slab_time = 0.5

MESH = pl.DeviceIdType.MESH


def lobatto_table():
    spread_root = math.sqrt(3.0 / 7.0)
    node_times = [0.0, (1.0 - spread_root) / 2.0, 0.5, (1.0 + spread_root) / 2.0, 1.0]
    table = [[0.0] * 5 for blank in range(5)]
    for column in range(5):
        coeffs = [1.0]
        divisor = 1.0
        for other_node in range(5):
            if other_node != column:
                product = [0.0] * (len(coeffs) + 1)
                for power, entry in enumerate(coeffs):
                    product[power + 1] += entry
                    product[power] -= node_times[other_node] * entry
                coeffs = product
                divisor *= node_times[column] - node_times[other_node]
        for row_index in range(5):
            upper = node_times[row_index]
            total_sum = 0.0
            for power, entry in enumerate(coeffs):
                total_sum += entry / (power + 1) * upper ** (power + 1)
            table[row_index][column] = total_sum / divisor
    return (np.array(node_times), np.array(table))


def rates(below, here, above, feed, drain):
    rows, lanes = here[0].shape

    def lap(i):
        w = here[i]
        around = (pltpu.roll(w, 1, 0) + pltpu.roll(w, rows - 1, 0)) + (
            pltpu.roll(w, 1, 1) + pltpu.roll(w, lanes - 1, 1)
        )
        return around + (below[i] + above[i]) - 6.0 * w

    s, c = here
    reacting = s * c * c
    grow_sub = substrate_spread * lap(0) - reacting + feed * (1.0 - s)
    grow_cat = catalyst_spread * lap(1) + reacting - drain * c
    return grow_sub, grow_cat


def kernel(
    slabs, blocks, weights,
    guess, feed_in, kill_in,
    end_out, last_out, rate_out,
    u, last, inc, bay, feed, drain, fbuf,
    load_sem, fixed_sem, tm_send, tm_recv, halo_send, halo_recv, edge_send,
    inc_send, inc_recv, bay_send, bay_recv, cast_send, back_send, far_send, cast_recv,
):
    layers = guess.shape[2]
    rows = guess.shape[3]
    final = SWEEPS - 1
    tm = lax.axis_index("tm")
    sp = lax.axis_index("space")
    left = lax.rem(sp + blocks - 1, blocks)
    right = lax.rem(sp + 1, blocks)
    source = tm == slabs - 1
    not_source = tm < slabs - 1
    second = tm == slabs - 2
    odd = tm % 2
    detoured = tm == slabs - 3

    def layer_of(c):
        return jnp.where(c < 2, c * (layers - 1), c - 1)

    loads = [
        pltpu.make_async_copy(guess, u.at[0, :, :, pl.ds(1, layers)], load_sem.at[0]),
        pltpu.make_async_copy(feed_in, feed, load_sem.at[1]),
        pltpu.make_async_copy(kill_in, drain, load_sem.at[2]),
    ]

    def fixed(k):
        return pltpu.make_async_copy(guess.at[0], u.at[k, 0, :, pl.ds(1, layers)], fixed_sem.at[k - 1])

    barrier = pltpu.get_barrier_semaphore()
    jumps = (1, 2, 3, 2 * min(2, slabs // 2 - 1))
    greeted = sorted({n % slabs for n in jumps} | {-n % slabs for n in jumps})
    for hop in greeted:
        pl.semaphore_signal(barrier, inc=1, device_id={"tm": lax.rem(tm + hop, slabs)}, device_id_type=MESH)
    for side in (left, right):
        pl.semaphore_signal(barrier, inc=1, device_id={"space": side}, device_id_type=MESH)

    for load in loads:
        load.start()

    @pl.when(tm == 0)
    def _():
        for k in range(1, SWEEPS + 1):
            fixed(k).start()

    pl.semaphore_wait(barrier, len(greeted) + 2)

    def stream(k, c, src):
        return pltpu.make_async_remote_copy(
            src_ref=src,
            dst_ref=u.at[k + 1, 0, :, 1 + layer_of(c)],
            send_sem=tm_send.at[k],
            recv_sem=tm_recv.at[k, c],
            device_id={"tm": lax.rem(tm + 1, slabs)},
            device_id_type=MESH,
        )

    def detour(k, c):
        return pltpu.make_async_remote_copy(
            src_ref=u.at[k, 4, :, 1 + layer_of(c)],
            dst_ref=bay.at[k // 2, :, layer_of(c)],
            send_sem=tm_send.at[k],
            recv_sem=bay_recv.at[k // 2, c],
            device_id={"tm": 0},
            device_id_type=MESH,
        )

    def onward(k, c):
        return pltpu.make_async_remote_copy(
            src_ref=bay.at[k // 2, :, layer_of(c)],
            dst_ref=u.at[k + 1, 0, :, 1 + layer_of(c)],
            send_sem=bay_send.at[k // 2],
            recv_sem=tm_recv.at[k, c],
            device_id={"tm": slabs - 2},
            device_id_type=MESH,
        )

    def aside(c):
        return pltpu.make_async_remote_copy(
            src_ref=guess.at[4, :, layer_of(c)],
            dst_ref=bay.at[0, :, layer_of(c)],
            send_sem=tm_send.at[0],
            recv_sem=bay_recv.at[0, c],
            device_id={"tm": slabs - 3},
            device_id_type=MESH,
        )

    def rejoin(c):
        return pltpu.make_async_remote_copy(
            src_ref=bay.at[0, :, layer_of(c)],
            dst_ref=u.at[1, 0, :, 1 + layer_of(c)],
            send_sem=bay_send.at[0],
            recv_sem=tm_recv.at[0, c],
            device_id={"tm": slabs - 1},
            device_id_type=MESH,
        )

    def halo(k, side, src):
        return pltpu.make_async_remote_copy(
            src_ref=src,
            dst_ref=u.at[k, :, :, (1 - side) * (layers + 1)],
            send_sem=halo_send,
            recv_sem=halo_recv.at[k, side],
            device_id={"space": left + side * (right - left)},
            device_id_type=MESH,
        )

    def own_edge(k, side):
        return u.at[k, :, :, 1 + side * (layers - 1)]

    halo(0, 0, guess.at[:, :, 0]).start()
    halo(0, 1, guess.at[:, :, layers - 1]).start()

    @pl.when(second)
    def _():
        @pl.loop(layers - SIDE, layers)
        def _(c):
            aside(c).start()

    @pl.when(not_source)
    def _():
        @pl.loop(0, jnp.where(second, layers - SIDE, layers))
        def _(c):
            stream(0, c, guess.at[4, :, layer_of(c)]).start()

    for load in loads:
        load.wait()
    drain[...] = drain[...] + feed[...]

    @pl.when(tm == 0)
    def _():
        for k in range(1, SWEEPS + 1):
            fixed(k).wait()

    def arrive(k, c):
        @pl.when(c == 0)
        def _():
            halo(k, 1, own_edge(k, 1)).wait_recv()

        @pl.when(c == 1)
        def _():
            halo(k, 0, own_edge(k, 0)).wait_recv()

    def begin(k, c):
        @pl.when(tm > 0)
        def _():
            stream(k, c, u.at[k, 4, :, 1 + layer_of(c)]).wait_recv()

    def all_rates(k, i):
        f, d = feed[i], drain[i]
        for j in range(5):
            below, here, above = ((u[k, j, 0, i + n], u[k, j, 1, i + n]) for n in range(3))
            fbuf[j, 0], fbuf[j, 1] = rates(below, here, above, f, d)

    def growth(grown, m):
        total = grown[0] * weights[m][0]
        for j in range(1, 5):
            total = total + grown[j] * weights[m][j]
        return total

    def step(k, i, nodes):
        @pl.loop(0, rows // 8)
        def _(r):
            at = pl.ds(pl.multiple_of(r * 8, 8), 8)
            for s in range(2):
                start = u[k + 1, 0, s, 1 + i, at]
                grown = [fbuf[j, s, at] for j in range(5)]
                for m in nodes:
                    u[k + 1, m, s, 1 + i, at] = start + growth(grown, m)

    def send_inc(c):
        at = inc.at[:, layer_of(c)]
        return pltpu.make_async_remote_copy(
            src_ref=at,
            dst_ref=at,
            send_sem=inc_send,
            recv_sem=inc_recv.at[c],
            device_id={"tm": slabs - 2},
            device_id_type=MESH,
        )

    def early(p):
        inner = jnp.where(p < layers - 3, p + 2, p - (layers - 3))
        return jnp.where(p < layers - 1, inner, p)

    def foresee(c):
        i = layer_of(c)
        arrive(final, c)
        all_rates(final, i)

        @pl.loop(0, rows // 8)
        def _(r):
            at = pl.ds(pl.multiple_of(r * 8, 8), 8)
            for s in range(2):
                inc[s, i, at] = growth([fbuf[j, s, at] for j in range(5)], 4)

        send_inc(c).start()

    depth = slabs // 2 - 1
    place = (slabs - 1 - tm) // 2
    entry = jnp.where(odd == 1, min(FIRST[1], depth), min(FIRST[0], depth))
    rooted = place == 0
    leads = rooted | ((place >= entry) & (place < depth))
    backs = (place >= 2) & (place <= entry)

    def cast(s, c, send, hop):
        at = last.at[s, 1 + layer_of(c)]
        return pltpu.make_async_remote_copy(
            src_ref=at,
            dst_ref=at,
            send_sem=send,
            recv_sem=cast_recv.at[s, c],
            device_id={"tm": lax.rem(tm + slabs + hop, slabs)},
            device_id_type=MESH,
        )

    def down(s, c):
        return cast(s, c, cast_send, jnp.where(rooted, -2 * entry, -2))

    def back(s, c):
        return cast(s, c, back_send, 2)

    paired = slabs >= 8 and min(FIRST[0], depth) == 2
    near = NEAR if paired else 0
    deep = DEEP if paired else 0
    spares_down = (tm == 3) | (tm == slabs - 3)
    spares_back = tm == slabs - 6

    def nearby(c):
        return c >= layers - near

    def offside(c):
        return (c < deep) | (c >= layers - deep // 2)

    def across(s, c):
        return cast(s, c, far_send, jnp.where(odd == 0, 1, -1))

    def last_halo(side):
        return pltpu.make_async_remote_copy(
            src_ref=last.at[:, 1 + side * (layers - 1)],
            dst_ref=last.at[:, (1 - side) * (layers + 1)],
            send_sem=edge_send,
            recv_sem=halo_recv.at[SWEEPS, side],
            device_id={"space": left + side * (right - left)},
            device_id_type=MESH,
        )

    plain = jnp.where((tm == slabs - 4) & paired, 1, odd)

    def chunk(p):
        return jnp.where(plain == 1, p, early(p))

    def relay(p):
        c = chunk(p)
        for s in range(2):
            @pl.when(tm < slabs - 2)
            def _():
                down(s, c).wait_recv()

            @pl.when(leads & jnp.logical_not(spares_down & nearby(c)))
            def _():
                down(s, c).start()

            @pl.when(backs & jnp.logical_not(spares_back & offside(c)))
            def _():
                back(s, c).start()

            @pl.when((((tm == 0) | (tm == slabs - 6)) & nearby(c)) | ((tm == slabs - 3) & offside(c)))
            def _():
                across(s, c).start()

        @pl.when(c == 0)
        def _():
            last_halo(0).start()

        @pl.when(c == 1)
        def _():
            last_halo(1).start()

    @pl.when(detoured)
    def _():
        @pl.loop(layers - SIDE, layers)
        def _(c):
            aside(c).wait_recv()
            rejoin(c).start()

    @pl.loop(0, final)
    def _(k):
        @pl.loop(0, layers)
        def _(c):
            i = layer_of(c)

            arrive(k, c)
            all_rates(k, i)
            begin(k, c)
            step(k, i, (4, 1, 2, 3))
            away = detoured & ((k == final - 1) | ((k == 0) & (c >= layers // 2)))


            @pl.when(not_source & jnp.logical_not(away))
            def _():
                stream(k + 1, c, u.at[k + 1, 4, :, 1 + i]).start()

            @pl.when(away)
            def _():
                detour(k + 1, c).start()

            @pl.when(c < 2)
            def _():
                halo(k + 1, c, own_edge(k + 1, c)).start()

            @pl.when((tm == 0) & (k == 0) & (c == layers - 1))
            def _():
                @pl.loop(layers // 2, layers)
                def _(b):
                    detour(1, b).wait_recv()
                    onward(1, b).start()

            @pl.when(source & (k == final - 1) & (c >= 3))
            def _():
                @pl.loop(c - 3, jnp.where(c == layers - 1, layers - 1, c - 2))
                def _(p):
                    foresee(early(p))

    steps = 1 + jnp.where(place > entry, place - entry, entry - place)
    lag = jnp.where(tm == 0, layers, jnp.minimum(2 * steps - 2 + 2 * odd, layers))

    def last_rate(c):
        i = layer_of(c)
        below, here, above = ((last[0, i + n], last[1, i + n]) for n in range(3))
        grow = rates(below, here, above, feed[i], drain[i])
        for s in range(2):
            last_out[s, i] = here[s]
            rate_out[s, i] = slab_time * grow[s]

    def settled(j):
        swapped = jnp.where(j < 3, j + 3, jnp.where(j < 4, 2, j + 2))
        return jnp.where(plain == 1, j + 2, swapped)

    @pl.when(tm == 0)
    def _():
        @pl.loop(0, layers)
        def _(c):
            detour(final, c).wait_recv()
            onward(final, c).start()

    @pl.when(second)
    def _():
        @pl.loop(0, layers)
        def _(p):
            i = layer_of(early(p))
            send_inc(early(p)).wait_recv()
            last[:, 1 + i] = u[final, 4, :, 1 + i] + inc[:, i]
            relay(p)

    ready = jnp.where(tm < slabs - 2, layers - 4, 0)

    @pl.loop(0, 2 * layers)
    def _(t):
        p = t - lag

        @pl.when((tm < slabs - 2) & (p >= 0) & (p < layers))
        def _():
            relay(p)

            @pl.when((p >= 2 + plain) & (p < layers - 2 + plain))
            def _():
                last_rate(settled(p - 2 - plain))

        @pl.when(not_source & (t < layers))
        def _():
            i = layer_of(t)
            arrive(final, t)
            all_rates(final, i)
            begin(final, t)
            step(final, i, (4,))
            end_out[:, i] = u[SWEEPS, 4, :, 1 + i]

        @pl.when(source & (t < layers))
        def _():
            i = layer_of(t)

            @pl.when(t == 2)
            def _():
                foresee(layers - 1)

            begin(final, t)
            now = u[SWEEPS, 0, :, 1 + i] + inc[:, i]
            last[:, 1 + i] = now
            end_out[:, i] = now
            relay(t)

    @pl.loop(ready, layers - 2)
    def _(j):
        last_rate(settled(j))

    last_halo(0).wait_recv()
    last_halo(1).wait_recv()

    @pl.loop(0, 2)
    def _(c):
        last_rate(c)

    def drain_sends(ref, sem):
        pltpu.make_async_copy(ref, ref, sem).wait()

    drain_sends(u.at[pl.ds(0, SWEEPS), :, :, pl.ds(1, 2)], halo_send)
    drain_sends(last.at[:, pl.ds(1, 2)], edge_send)
    whole = last.at[:, pl.ds(1, layers)]

    @pl.when(not_source)
    def _():
        for k in range(SWEEPS):
            drain_sends(whole, tm_send.at[k])

    @pl.when(source)
    def _():
        drain_sends(whole, inc_send)

    @pl.when(detoured)
    def _():
        drain_sends(last.at[:, pl.ds(1, SIDE)], bay_send.at[0])

    @pl.when(tm == 0)
    def _():
        drain_sends(whole, bay_send.at[1])
        drain_sends(last.at[:, pl.ds(1, layers - layers // 2)], bay_send.at[0])

    @pl.when(leads & jnp.logical_not(spares_down))
    def _():
        drain_sends(whole, cast_send)

    @pl.when(leads & spares_down)
    def _():
        drain_sends(last.at[:, pl.ds(1, layers - near)], cast_send)

    @pl.when(backs & jnp.logical_not(spares_back))
    def _():
        drain_sends(whole, back_send)

    @pl.when(backs & spares_back)
    def _():
        drain_sends(last.at[:, pl.ds(1, layers - deep - deep // 2)], back_send)

    if paired:
        @pl.when((tm == 0) | (tm == slabs - 6))
        def _():
            drain_sends(last.at[:, pl.ds(1, near)], far_send)

        @pl.when(tm == slabs - 3)
        def _():
            drain_sends(last.at[:, pl.ds(1, deep + deep // 2)], far_send)


def finish(offsets, end, last, rate, end_hbm, next_hbm, nodes, sems, start_sem, end_sem):
    layers = end.shape[1]
    start_copy = pltpu.make_async_copy(last, next_hbm.at[0], start_sem)
    end_copy = pltpu.make_async_copy(end, end_hbm, end_sem)
    start_copy.start()
    end_copy.start()

    def out(i):
        return pltpu.make_async_copy(nodes.at[:, :, i], next_hbm.at[pl.ds(1, 4), :, i], sems.at[i])

    for i in range(layers):
        for s in range(2):
            base = last[s, i]
            grow = rate[s, i]
            for m in range(1, 5):
                nodes[m - 1, s, i] = base + offsets[m] * grow
        out(i).start()
    for i in range(layers):
        out(i).wait()
    start_copy.wait()
    end_copy.wait()


def shards(slabs, blocks, guess, feed_rate, kill_rate):
    node_times, table = lobatto_table()
    weights = [[float(np.float32(slab_time * w)) for w in row] for row in table]
    offsets = [float(np.float32(t)) for t in node_times]
    _, nodes, species, layers, rows, lanes = guess.shape
    pair = jax.ShapeDtypeStruct((species, layers, rows, lanes), jnp.float32)
    dma = pltpu.SemaphoreType.DMA
    vmem = pl.BlockSpec(memory_space=pltpu.VMEM)
    hbm = pl.BlockSpec(memory_space=pltpu.HBM)
    end, last, rate = pl.pallas_call(
        functools.partial(kernel, slabs, blocks, weights),
        out_shape=(pair,) * 3,
        in_specs=[hbm] * 3,
        out_specs=(vmem,) * 3,
        scratch_shapes=[
            pltpu.VMEM((SWEEPS + 1, nodes, species, layers + 2, rows, lanes), jnp.float32),
            pltpu.VMEM((species, layers + 2, rows, lanes), jnp.float32),
            pltpu.VMEM((species, layers, rows, lanes), jnp.float32),
            pltpu.VMEM((2, species, layers, rows, lanes), jnp.float32),
            pltpu.VMEM((layers, rows, lanes), jnp.float32),
            pltpu.VMEM((layers, rows, lanes), jnp.float32),
            pltpu.VMEM((nodes, species, rows, lanes), jnp.float32),
            dma((3,)),
            dma((SWEEPS,)),
            dma((SWEEPS,)),
            dma((SWEEPS, layers)),
            dma(()),
            dma((SWEEPS + 1, 2)),
            dma(()),
            dma(()),
            dma((layers,)),
            dma((2,)),
            dma((2, layers)),
            dma(()),
            dma(()),
            dma(()),
            dma((species, layers)),
        ],
        compiler_params=pltpu.CompilerParams(
            collective_id=0, has_side_effects=True, vmem_limit_bytes=40 * 1024 * 1024
        ),
    )(*(pltpu.with_memory_space_constraint(x, pltpu.HBM) for x in (guess[0], feed_rate, kill_rate)))
    end_state, next_nodes = pl.pallas_call(
        functools.partial(finish, offsets),
        out_shape=(pair, jax.ShapeDtypeStruct((nodes, species, layers, rows, lanes), jnp.float32)),
        in_specs=[vmem] * 3,
        out_specs=(hbm, hbm),
        scratch_shapes=[
            pltpu.VMEM((nodes - 1, species, layers, rows, lanes), jnp.float32),
            dma((layers,)),
            dma(()),
            dma(()),
        ],
        compiler_params=pltpu.CompilerParams(vmem_limit_bytes=16 * 1024 * 1024),
    )(end, last, rate)
    return (end_state[None], next_nodes[None])


def solution(mesh):
    placed = (
        P("tm", None, None, "space", None, None),
        P("space", None, None),
        P("space", None, None),
    )
    return jax.shard_map(
        functools.partial(shards, mesh.shape["tm"], mesh.shape["space"]),
        mesh=mesh,
        in_specs=placed,
        out_specs=(P("tm", None, "space", None, None), P("tm", None, None, "space", None, None)),
        check_vma=False,
    )
```

```python
import functools
import math

import jax
import jax.numpy as jnp
import numpy as np
from jax import lax
from jax.experimental import pallas as pl
from jax.experimental.pallas import tpu as pltpu
from jax.sharding import PartitionSpec as P

SWEEPS = 4
SIDE = 1
FIRST = (2, 1)
NEAR = 4
DEEP = 2

substrate_spread = 0.2
catalyst_spread = 0.1
slab_time = 0.5

MESH = pl.DeviceIdType.MESH


def lobatto_table():
    spread_root = math.sqrt(3.0 / 7.0)
    node_times = [0.0, (1.0 - spread_root) / 2.0, 0.5, (1.0 + spread_root) / 2.0, 1.0]
    table = [[0.0] * 5 for blank in range(5)]
    for column in range(5):
        coeffs = [1.0]
        divisor = 1.0
        for other_node in range(5):
            if other_node != column:
                product = [0.0] * (len(coeffs) + 1)
                for power, entry in enumerate(coeffs):
                    product[power + 1] += entry
                    product[power] -= node_times[other_node] * entry
                coeffs = product
                divisor *= node_times[column] - node_times[other_node]
        for row_index in range(5):
            upper = node_times[row_index]
            total_sum = 0.0
            for power, entry in enumerate(coeffs):
                total_sum += entry / (power + 1) * upper ** (power + 1)
            table[row_index][column] = total_sum / divisor
    return (np.array(node_times), np.array(table))


def rates(below, here, above, feed, drain):
    rows, lanes = here[0].shape

    def lap(i):
        w = here[i]
        around = (pltpu.roll(w, 1, 0) + pltpu.roll(w, rows - 1, 0)) + (
            pltpu.roll(w, 1, 1) + pltpu.roll(w, lanes - 1, 1)
        )
        return around + (below[i] + above[i]) - 6.0 * w

    s, c = here
    reacting = s * c * c
    grow_sub = substrate_spread * lap(0) - reacting + feed * (1.0 - s)
    grow_cat = catalyst_spread * lap(1) + reacting - drain * c
    return grow_sub, grow_cat


def kernel(
    slabs, blocks, weights,
    guess, feed_in, kill_in,
    end_out, last_out, rate_out,
    u, last, inc, bay, feed, drain, fbuf,
    load_sem, fixed_sem, tm_send, tm_recv, halo_send, halo_recv, edge_send,
    inc_send, inc_recv, bay_send, bay_recv, cast_send, back_send, far_send, cast_recv,
):
    layers = guess.shape[2]
    rows = guess.shape[3]
    final = SWEEPS - 1
    tm = lax.axis_index("tm")
    sp = lax.axis_index("space")
    left = lax.rem(sp + blocks - 1, blocks)
    right = lax.rem(sp + 1, blocks)
    source = tm == slabs - 1
    not_source = tm < slabs - 1
    second = tm == slabs - 2
    odd = tm % 2
    detoured = tm == slabs - 3

    def layer_of(c):
        return jnp.where(c < 2, c * (layers - 1), c - 1)

    loads = [
        pltpu.make_async_copy(guess, u.at[0, :, :, pl.ds(1, layers)], load_sem.at[0]),
        pltpu.make_async_copy(feed_in, feed, load_sem.at[1]),
        pltpu.make_async_copy(kill_in, drain, load_sem.at[2]),
    ]

    def fixed(k):
        return pltpu.make_async_copy(guess.at[0], u.at[k, 0, :, pl.ds(1, layers)], fixed_sem.at[k - 1])

    barrier = pltpu.get_barrier_semaphore()
    jumps = (1, 2, 3, 2 * min(2, slabs // 2 - 1))
    greeted = sorted({n % slabs for n in jumps} | {-n % slabs for n in jumps})
    for hop in greeted:
        pl.semaphore_signal(barrier, inc=1, device_id={"tm": lax.rem(tm + hop, slabs)}, device_id_type=MESH)
    for side in (left, right):
        pl.semaphore_signal(barrier, inc=1, device_id={"space": side}, device_id_type=MESH)

    for load in loads:
        load.start()

    @pl.when(tm == 0)
    def _():
        for k in range(1, SWEEPS + 1):
            fixed(k).start()

    pl.semaphore_wait(barrier, len(greeted) + 2)

    def stream(k, c, src):
        return pltpu.make_async_remote_copy(
            src_ref=src,
            dst_ref=u.at[k + 1, 0, :, 1 + layer_of(c)],
            send_sem=tm_send.at[k],
            recv_sem=tm_recv.at[k, c],
            device_id={"tm": lax.rem(tm + 1, slabs)},
            device_id_type=MESH,
        )

    def detour(k, c):
        return pltpu.make_async_remote_copy(
            src_ref=u.at[k, 4, :, 1 + layer_of(c)],
            dst_ref=bay.at[k // 2, :, layer_of(c)],
            send_sem=tm_send.at[k],
            recv_sem=bay_recv.at[k // 2, c],
            device_id={"tm": 0},
            device_id_type=MESH,
        )

    def onward(k, c):
        return pltpu.make_async_remote_copy(
            src_ref=bay.at[k // 2, :, layer_of(c)],
            dst_ref=u.at[k + 1, 0, :, 1 + layer_of(c)],
            send_sem=bay_send.at[k // 2],
            recv_sem=tm_recv.at[k, c],
            device_id={"tm": slabs - 2},
            device_id_type=MESH,
        )

    def aside(c):
        return pltpu.make_async_remote_copy(
            src_ref=guess.at[4, :, layer_of(c)],
            dst_ref=bay.at[0, :, layer_of(c)],
            send_sem=tm_send.at[0],
            recv_sem=bay_recv.at[0, c],
            device_id={"tm": slabs - 3},
            device_id_type=MESH,
        )

    def rejoin(c):
        return pltpu.make_async_remote_copy(
            src_ref=bay.at[0, :, layer_of(c)],
            dst_ref=u.at[1, 0, :, 1 + layer_of(c)],
            send_sem=bay_send.at[0],
            recv_sem=tm_recv.at[0, c],
            device_id={"tm": slabs - 1},
            device_id_type=MESH,
        )

    def halo(k, side, src):
        return pltpu.make_async_remote_copy(
            src_ref=src,
            dst_ref=u.at[k, :, :, (1 - side) * (layers + 1)],
            send_sem=halo_send,
            recv_sem=halo_recv.at[k, side],
            device_id={"space": left + side * (right - left)},
            device_id_type=MESH,
        )

    def own_edge(k, side):
        return u.at[k, :, :, 1 + side * (layers - 1)]

    halo(0, 0, guess.at[:, :, 0]).start()
    halo(0, 1, guess.at[:, :, layers - 1]).start()

    @pl.when(second)
    def _():
        @pl.loop(layers - SIDE, layers)
        def _(c):
            aside(c).start()

    @pl.when(not_source)
    def _():
        @pl.loop(0, jnp.where(second, layers - SIDE, layers))
        def _(c):
            stream(0, c, guess.at[4, :, layer_of(c)]).start()

    for load in loads:
        load.wait()
    drain[...] = drain[...] + feed[...]

    @pl.when(tm == 0)
    def _():
        for k in range(1, SWEEPS + 1):
            fixed(k).wait()

    def arrive(k, c):
        @pl.when(c == 0)
        def _():
            halo(k, 1, own_edge(k, 1)).wait_recv()

        @pl.when(c == 1)
        def _():
            halo(k, 0, own_edge(k, 0)).wait_recv()

    def begin(k, c):
        @pl.when(tm > 0)
        def _():
            stream(k, c, u.at[k, 4, :, 1 + layer_of(c)]).wait_recv()

    def all_rates(k, i):
        f, d = feed[i], drain[i]
        for j in range(5):
            below, here, above = ((u[k, j, 0, i + n], u[k, j, 1, i + n]) for n in range(3))
            fbuf[j, 0], fbuf[j, 1] = rates(below, here, above, f, d)

    def growth(grown, m):
        total = grown[0] * weights[m][0]
        for j in range(1, 5):
            total = total + grown[j] * weights[m][j]
        return total

    def step(k, i, nodes):
        @pl.loop(0, rows // 8)
        def _(r):
            at = pl.ds(pl.multiple_of(r * 8, 8), 8)
            for s in range(2):
                start = u[k + 1, 0, s, 1 + i, at]
                grown = [fbuf[j, s, at] for j in range(5)]
                for m in nodes:
                    u[k + 1, m, s, 1 + i, at] = start + growth(grown, m)

    def send_inc(c):
        at = inc.at[:, layer_of(c)]
        return pltpu.make_async_remote_copy(
            src_ref=at,
            dst_ref=at,
            send_sem=inc_send,
            recv_sem=inc_recv.at[c],
            device_id={"tm": slabs - 2},
            device_id_type=MESH,
        )

    def early(p):
        inner = jnp.where(p < layers - 3, p + 2, p - (layers - 3))
        return jnp.where(p < layers - 1, inner, p)

    def foresee(c):
        i = layer_of(c)
        arrive(final, c)
        all_rates(final, i)

        @pl.loop(0, rows // 8)
        def _(r):
            at = pl.ds(pl.multiple_of(r * 8, 8), 8)
            for s in range(2):
                inc[s, i, at] = growth([fbuf[j, s, at] for j in range(5)], 4)

        send_inc(c).start()

    depth = slabs // 2 - 1
    place = (slabs - 1 - tm) // 2
    entry = jnp.where(odd == 1, min(FIRST[1], depth), min(FIRST[0], depth))
    rooted = place == 0
    leads = rooted | ((place >= entry) & (place < depth))
    backs = (place >= 2) & (place <= entry)

    def cast(s, c, send, hop):
        at = last.at[s, 1 + layer_of(c)]
        return pltpu.make_async_remote_copy(
            src_ref=at,
            dst_ref=at,
            send_sem=send,
            recv_sem=cast_recv.at[s, c],
            device_id={"tm": lax.rem(tm + slabs + hop, slabs)},
            device_id_type=MESH,
        )

    def down(s, c):
        return cast(s, c, cast_send, jnp.where(rooted, -2 * entry, -2))

    def back(s, c):
        return cast(s, c, back_send, 2)

    paired = slabs >= 8 and min(FIRST[0], depth) == 2
    near = NEAR if paired else 0
    deep = DEEP if paired else 0
    spares_down = (tm == 3) | (tm == slabs - 3)
    spares_back = tm == slabs - 6

    def nearby(c):
        return c >= layers - near

    def offside(c):
        return c < deep

    def across(s, c):
        return cast(s, c, far_send, jnp.where(odd == 0, 1, -1))

    def last_halo(side):
        return pltpu.make_async_remote_copy(
            src_ref=last.at[:, 1 + side * (layers - 1)],
            dst_ref=last.at[:, (1 - side) * (layers + 1)],
            send_sem=edge_send,
            recv_sem=halo_recv.at[SWEEPS, side],
            device_id={"space": left + side * (right - left)},
            device_id_type=MESH,
        )

    plain = jnp.where((tm == slabs - 4) & paired, 1, odd)

    def chunk(p):
        return jnp.where(plain == 1, p, early(p))

    def relay(p):
        c = chunk(p)
        for s in range(2):
            @pl.when(tm < slabs - 2)
            def _():
                down(s, c).wait_recv()

            @pl.when(leads & jnp.logical_not(spares_down & nearby(c)))
            def _():
                down(s, c).start()

            @pl.when(backs & jnp.logical_not(spares_back & offside(c)))
            def _():
                back(s, c).start()

            @pl.when((((tm == 0) | (tm == slabs - 6)) & nearby(c)) | ((tm == slabs - 3) & offside(c)))
            def _():
                across(s, c).start()

        @pl.when(c == 0)
        def _():
            last_halo(0).start()

        @pl.when(c == 1)
        def _():
            last_halo(1).start()

    @pl.when(detoured)
    def _():
        @pl.loop(layers - SIDE, layers)
        def _(c):
            aside(c).wait_recv()
            rejoin(c).start()

    @pl.loop(0, final)
    def _(k):
        @pl.loop(0, layers)
        def _(c):
            i = layer_of(c)

            arrive(k, c)
            all_rates(k, i)
            begin(k, c)
            step(k, i, (4, 1, 2, 3))
            away = detoured & ((k == final - 1) | ((k == 0) & (c >= layers // 2)))


            @pl.when(not_source & jnp.logical_not(away))
            def _():
                stream(k + 1, c, u.at[k + 1, 4, :, 1 + i]).start()

            @pl.when(away)
            def _():
                detour(k + 1, c).start()

            @pl.when(c < 2)
            def _():
                halo(k + 1, c, own_edge(k + 1, c)).start()

            @pl.when((tm == 0) & (k == 0) & (c == layers - 1))
            def _():
                @pl.loop(layers // 2, layers)
                def _(b):
                    detour(1, b).wait_recv()
                    onward(1, b).start()

            @pl.when(source & (k == final - 1) & (c >= 3))
            def _():
                @pl.loop(c - 3, jnp.where(c == layers - 1, layers - 1, c - 2))
                def _(p):
                    foresee(early(p))

    steps = 1 + jnp.where(place > entry, place - entry, entry - place)
    lag = jnp.where(tm == 0, layers, jnp.minimum(2 * steps - 2 + 2 * odd, layers))

    def last_rate(c):
        i = layer_of(c)
        below, here, above = ((last[0, i + n], last[1, i + n]) for n in range(3))
        grow = rates(below, here, above, feed[i], drain[i])
        for s in range(2):
            last_out[s, i] = here[s]
            rate_out[s, i] = slab_time * grow[s]

    def settled(j):
        swapped = jnp.where(j < 3, j + 3, jnp.where(j < 4, 2, j + 2))
        return jnp.where(plain == 1, j + 2, swapped)

    @pl.when(tm == 0)
    def _():
        @pl.loop(0, layers)
        def _(c):
            detour(final, c).wait_recv()
            onward(final, c).start()

    @pl.when(second)
    def _():
        @pl.loop(0, layers)
        def _(p):
            i = layer_of(early(p))
            send_inc(early(p)).wait_recv()
            last[:, 1 + i] = u[final, 4, :, 1 + i] + inc[:, i]
            relay(p)

    ready = jnp.where(tm < slabs - 2, layers - 4, 0)

    @pl.loop(0, 2 * layers)
    def _(t):
        p = t - lag

        @pl.when((tm < slabs - 2) & (p >= 0) & (p < layers))
        def _():
            relay(p)

            @pl.when((p >= 2 + plain) & (p < layers - 2 + plain))
            def _():
                last_rate(settled(p - 2 - plain))

        @pl.when(not_source & (t < layers))
        def _():
            i = layer_of(t)
            arrive(final, t)
            all_rates(final, i)
            begin(final, t)
            step(final, i, (4,))
            end_out[:, i] = u[SWEEPS, 4, :, 1 + i]

        @pl.when(source & (t < layers))
        def _():
            i = layer_of(t)

            @pl.when(t == 2)
            def _():
                foresee(layers - 1)

            begin(final, t)
            now = u[SWEEPS, 0, :, 1 + i] + inc[:, i]
            last[:, 1 + i] = now
            end_out[:, i] = now
            relay(t)

    @pl.loop(ready, layers - 2)
    def _(j):
        last_rate(settled(j))

    last_halo(0).wait_recv()
    last_halo(1).wait_recv()

    @pl.loop(0, 2)
    def _(c):
        last_rate(c)

    def drain_sends(ref, sem):
        pltpu.make_async_copy(ref, ref, sem).wait()

    drain_sends(u.at[pl.ds(0, SWEEPS), :, :, pl.ds(1, 2)], halo_send)
    drain_sends(last.at[:, pl.ds(1, 2)], edge_send)
    whole = last.at[:, pl.ds(1, layers)]

    @pl.when(not_source)
    def _():
        for k in range(SWEEPS):
            drain_sends(whole, tm_send.at[k])

    @pl.when(source)
    def _():
        drain_sends(whole, inc_send)

    @pl.when(detoured)
    def _():
        drain_sends(last.at[:, pl.ds(1, SIDE)], bay_send.at[0])

    @pl.when(tm == 0)
    def _():
        drain_sends(whole, bay_send.at[1])
        drain_sends(last.at[:, pl.ds(1, layers - layers // 2)], bay_send.at[0])

    @pl.when(leads & jnp.logical_not(spares_down))
    def _():
        drain_sends(whole, cast_send)

    @pl.when(leads & spares_down)
    def _():
        drain_sends(last.at[:, pl.ds(1, layers - near)], cast_send)

    @pl.when(backs & jnp.logical_not(spares_back))
    def _():
        drain_sends(whole, back_send)

    @pl.when(backs & spares_back)
    def _():
        drain_sends(last.at[:, pl.ds(1, layers - deep)], back_send)

    if paired:
        @pl.when((tm == 0) | (tm == slabs - 6))
        def _():
            drain_sends(last.at[:, pl.ds(1, near)], far_send)

        @pl.when(tm == slabs - 3)
        def _():
            drain_sends(last.at[:, pl.ds(1, deep)], far_send)


def finish(offsets, end, last, rate, end_hbm, next_hbm, nodes, sems, start_sem, end_sem):
    layers = end.shape[1]
    start_copy = pltpu.make_async_copy(last, next_hbm.at[0], start_sem)
    end_copy = pltpu.make_async_copy(end, end_hbm, end_sem)
    start_copy.start()
    end_copy.start()

    def out(i):
        return pltpu.make_async_copy(nodes.at[:, :, i], next_hbm.at[pl.ds(1, 4), :, i], sems.at[i])

    for i in range(layers):
        for s in range(2):
            base = last[s, i]
            grow = rate[s, i]
            for m in range(1, 5):
                nodes[m - 1, s, i] = base + offsets[m] * grow
        out(i).start()
    for i in range(layers):
        out(i).wait()
    start_copy.wait()
    end_copy.wait()


def shards(slabs, blocks, guess, feed_rate, kill_rate):
    node_times, table = lobatto_table()
    weights = [[float(np.float32(slab_time * w)) for w in row] for row in table]
    offsets = [float(np.float32(t)) for t in node_times]
    _, nodes, species, layers, rows, lanes = guess.shape
    pair = jax.ShapeDtypeStruct((species, layers, rows, lanes), jnp.float32)
    dma = pltpu.SemaphoreType.DMA
    vmem = pl.BlockSpec(memory_space=pltpu.VMEM)
    hbm = pl.BlockSpec(memory_space=pltpu.HBM)
    end, last, rate = pl.pallas_call(
        functools.partial(kernel, slabs, blocks, weights),
        out_shape=(pair,) * 3,
        in_specs=[hbm] * 3,
        out_specs=(vmem,) * 3,
        scratch_shapes=[
            pltpu.VMEM((SWEEPS + 1, nodes, species, layers + 2, rows, lanes), jnp.float32),
            pltpu.VMEM((species, layers + 2, rows, lanes), jnp.float32),
            pltpu.VMEM((species, layers, rows, lanes), jnp.float32),
            pltpu.VMEM((2, species, layers, rows, lanes), jnp.float32),
            pltpu.VMEM((layers, rows, lanes), jnp.float32),
            pltpu.VMEM((layers, rows, lanes), jnp.float32),
            pltpu.VMEM((nodes, species, rows, lanes), jnp.float32),
            dma((3,)),
            dma((SWEEPS,)),
            dma((SWEEPS,)),
            dma((SWEEPS, layers)),
            dma(()),
            dma((SWEEPS + 1, 2)),
            dma(()),
            dma(()),
            dma((layers,)),
            dma((2,)),
            dma((2, layers)),
            dma(()),
            dma(()),
            dma(()),
            dma((species, layers)),
        ],
        compiler_params=pltpu.CompilerParams(
            collective_id=0, has_side_effects=True, vmem_limit_bytes=40 * 1024 * 1024
        ),
    )(*(pltpu.with_memory_space_constraint(x, pltpu.HBM) for x in (guess[0], feed_rate, kill_rate)))
    end_state, next_nodes = pl.pallas_call(
        functools.partial(finish, offsets),
        out_shape=(pair, jax.ShapeDtypeStruct((nodes, species, layers, rows, lanes), jnp.float32)),
        in_specs=[vmem] * 3,
        out_specs=(hbm, hbm),
        scratch_shapes=[
            pltpu.VMEM((nodes - 1, species, layers, rows, lanes), jnp.float32),
            dma((layers,)),
            dma(()),
            dma(()),
        ],
        compiler_params=pltpu.CompilerParams(vmem_limit_bytes=16 * 1024 * 1024),
    )(end, last, rate)
    return (end_state[None], next_nodes[None])


def solution(mesh):
    placed = (
        P("tm", None, None, "space", None, None),
        P("space", None, None),
        P("space", None, None),
    )
    return jax.shard_map(
        functools.partial(shards, mesh.shape["tm"], mesh.shape["space"]),
        mesh=mesh,
        in_specs=placed,
        out_specs=(P("tm", None, "space", None, None), P("tm", None, None, "space", None, None)),
        check_vma=False,
    )
```
